128 devices in a mesh: gz: 4 (over z), gy: 8 (over y, core), gx: 4 (over x).
Axes of the slice: x: 4, y: 4, z: 4, core: 2. Of those that a mesh axis runs over, the one named last changes fastest.
Arguments:
- ref_image: float32 [64, 512, 512], P('gz', 'gy', 'gx'), may hold values from -40 to 40
- deformed_image: float32 [64, 512, 512], P('gz', 'gy', 'gx'), may hold values from -40 to 40
- nodal_disp: int32 [3, 8, 40, 36], P(None, 'gz', 'gy', 'gx'), may hold values from -1024 to 1023, as said below
Outputs:
- update: float32 [3, 8, 40, 36], P(None, 'gz', 'gy', 'gx')
- cg_residual: float32 [3, 8, 40, 36], P(None, 'gz', 'gy', 'gx')
The draws below stay inside these ranges and needn't reach their ends.
Inputs may be any that keep to these rules, and one draw needn't show every extreme that they name: `nodal_disp`: copies of a node held by neighbouring bricks are equal.
All inputs are finite; a program needn't handle non-finite values.
Results may differ from the reference program's by a relative error of at most 0.0003.
Values sent between devices are 32-bit elements; how exact they have to be, the bound alone decides.
No kernel may reach another device: no remote copies, remote signals or barrier semaphores. Data moves between devices by JAX's collectives and lax.ppermute only.
A program may use at most 256 MiB of HBM per device.

```python
import jax
import jax.numpy as jnp
import numpy as np
from jax import lax

ELEM = 16
EZ = 1
EY = 4
EX = 8
CGSTEPS = 8
NZ = 64
NY = 512
NX = 512
N_GZ = 4
N_GY = 8
N_GX = 4


def contrast():
    depth = jnp.arange(NZ, dtype=jnp.float32) / NZ
    across = jnp.arange(NY, dtype=jnp.float32) / NY
    along = jnp.arange(NX, dtype=jnp.float32) / NX
    return 10.0 ** ((depth[:, None, None] + across[None, :, None] + along[None, None, :]) / 3.0)


def draw_ref_image(key, part):
    key = jax.random.fold_in(key, 11)
    noise = jnp.clip(jax.random.normal(key, (NZ, NY, NX), jnp.float32), -3.5, 3.5)
    return contrast() * noise


def draw_deformed_image(key, part):
    key = jax.random.fold_in(key, 13)
    noise = jnp.clip(jax.random.normal(key, (NZ, NY, NX), jnp.float32), -3.5, 3.5)
    return contrast() * noise


def draw_nodal_disp(key, part):
    key = jax.random.fold_in(key, 17)
    first_key, second_key, third_key = jax.random.split(key, 3)
    nodes_z = EZ * N_GZ + 1
    nodes_y = EY * N_GY + 1
    nodes_x = EX * N_GX + 1
    field = jax.random.randint(first_key, (3, nodes_z, nodes_y, nodes_x), -1024, 1024, dtype=jnp.int32)
    flat = field.reshape(-1)
    middle = flat.shape[0] // 2
    lowest = jax.random.randint(second_key, (), 0, middle, dtype=jnp.int32)
    highest = jax.random.randint(third_key, (), middle, flat.shape[0], dtype=jnp.int32)
    flat = flat.at[lowest].set(-1024).at[highest].set(1023)
    field = flat.reshape((3, nodes_z, nodes_y, nodes_x))
    for axis, (groups, elems) in enumerate(((N_GZ, EZ), (N_GY, EY), (N_GX, EX))):
        index = (np.arange(groups)[:, None] * elems + np.arange(elems + 1)[None, :]).ravel()
        field = jnp.take(field, jnp.asarray(index, dtype=jnp.int32), axis=axis + 1)
    return field


def setup_inputs(seed: int = 0) -> dict:
    key_of = jax.random.split(jax.random.key(seed), 4)
    return {
        "ref_image": draw_ref_image(jax.random.fold_in(key_of[3], 71), 0),
        "deformed_image": draw_deformed_image(jax.random.fold_in(key_of[3], 71), 0),
        "nodal_disp": draw_nodal_disp(jax.random.fold_in(key_of[3], 71), 0),
    }


quantum = 64
damping = 0.5


def weights():
    position = (jnp.arange(ELEM, dtype=jnp.float32) + 0.5) / ELEM
    return jnp.stack([1.0 - position, position])


def corners(field):
    count_z, count_y, count_x = field.shape[1] - 1, field.shape[2] - 1, field.shape[3] - 1
    pieces = []
    for offset in range(8):
        along_z, along_y, along_x = offset >> 2, (offset >> 1) & 1, offset & 1
        pieces.append(field[:, along_z:along_z + count_z, along_y:along_y + count_y, along_x:along_x + count_x])
    return jnp.stack(pieces, axis=1).reshape((field.shape[0], 2, 2, 2, count_z, count_y, count_x))


def assemble(parts):
    total = 0.0
    for offset in range(8):
        along_z, along_y, along_x = offset >> 2, (offset >> 1) & 1, offset & 1
        total = total + jnp.pad(parts[:, along_z, along_y, along_x], ((0, 0), (along_z, 1 - along_z), (along_y, 1 - along_y), (along_x, 1 - along_x)))
    return total


def blocks(volume):
    lead = volume.shape[:-3]
    count_z, count_y, count_x = volume.shape[-3] // ELEM, volume.shape[-2] // ELEM, volume.shape[-1] // ELEM
    shaped = volume.reshape(lead + (count_z, ELEM, count_y, ELEM, count_x, ELEM))
    number = len(lead)
    order = tuple(range(number)) + (number + 1, number + 3, number + 5, number, number + 2, number + 4)
    return jnp.transpose(shaped, order).reshape(lead + (ELEM, ELEM, ELEM, count_z * count_y * count_x))


def element_terms(ref_pad, deformed_pad, nodes):
    count_z, count_y, count_x = nodes.shape[1] - 1, nodes.shape[2] - 1, nodes.shape[3] - 1
    image = ref_pad[1:-1, 1:-1, 1:-1]
    gradient = jnp.stack([
        0.5 * (ref_pad[2:, 1:-1, 1:-1] - ref_pad[:-2, 1:-1, 1:-1]),
        0.5 * (ref_pad[1:-1, 2:, 1:-1] - ref_pad[1:-1, :-2, 1:-1]),
        0.5 * (ref_pad[1:-1, 1:-1, 2:] - ref_pad[1:-1, 1:-1, :-2])])
    summed = jnp.sum(corners(nodes).reshape((3, 8, count_z, count_y, count_x)), axis=1)
    whole = jnp.floor_divide(summed, 8 * quantum)
    fraction = (summed - whole * (8 * quantum)).astype(jnp.float32) / (8.0 * quantum)
    anchor_z = jnp.arange(count_z, dtype=jnp.int32) * ELEM
    anchor_y = jnp.arange(count_y, dtype=jnp.int32) * ELEM
    anchor_x = jnp.arange(count_x, dtype=jnp.int32) * ELEM
    start_z = (anchor_z[:, None, None] + whole[0] + ELEM).reshape(-1).astype(jnp.int32)
    start_y = (anchor_y[None, :, None] + whole[1] + ELEM).reshape(-1).astype(jnp.int32)
    start_x = (anchor_x[None, None, :] + whole[2] + ELEM).reshape(-1).astype(jnp.int32)

    def cutout(first, second, third):
        return lax.dynamic_slice(deformed_pad, (first, second, third), (ELEM + 1, ELEM + 1, ELEM + 1))

    boxes = jax.vmap(cutout, out_axes=3)(start_z, start_y, start_x)
    shares = fraction.reshape((3, -1))
    warped = (1.0 - shares[0]) * boxes[:-1] + shares[0] * boxes[1:]
    warped = (1.0 - shares[1]) * warped[:, :-1] + shares[1] * warped[:, 1:]
    warped = (1.0 - shares[2]) * warped[:, :, :-1] + shares[2] * warped[:, :, 1:]
    mismatch = blocks(image) - warped
    slopes = blocks(gradient)
    shape_fn = weights()
    scale = 1.0 / ELEM ** 2
    rhs = jnp.einsum('cijkn,ai,bj,dk->cabdn', slopes * mismatch, shape_fn, shape_fn, shape_fn, precision=lax.Precision.HIGHEST) * scale
    double = shape_fn[:, None, :] * shape_fn[None, :, :]
    rows_list = []
    for component in range(3):
        rows_list.append(jnp.einsum('dijkn,api,bqj,grk->dabgpqrn', slopes[component] * slopes, double, double, double, precision=lax.Precision.HIGHEST) * scale)
    hessian = jnp.stack(rows_list).reshape((3, 3, 2, 2, 2, 2, 2, 2, count_z, count_y, count_x))
    return assemble(rhs.reshape((3, 2, 2, 2, count_z, count_y, count_x))), hessian


def apply_local(hessian, field):
    values = corners(field)
    result = jnp.einsum('cdabgpqrxyz,dpqrxyz->cabgxyz', hessian, values, precision=lax.Precision.HIGHEST)
    return assemble(result)


def unique_nodes(copies):
    for axis, (groups, elems) in enumerate(((N_GZ, EZ), (N_GY, EY), (N_GX, EX))):
        index = np.concatenate([(np.arange(groups)[:, None] * (elems + 1) + np.arange(elems)[None, :]).ravel(), np.array([groups * (elems + 1) - 1])])
        copies = jnp.take(copies, jnp.asarray(index, dtype=jnp.int32), axis=axis + 1)
    return copies


def expand_nodes(field):
    for axis, (groups, elems) in enumerate(((N_GZ, EZ), (N_GY, EY), (N_GX, EX))):
        index = (np.arange(groups)[:, None] * elems + np.arange(elems + 1)[None, :]).ravel()
        field = jnp.take(field, jnp.asarray(index, dtype=jnp.int32), axis=axis + 1)
    return field


def reference(ref_image, deformed_image, nodal_disp):
    nodes = unique_nodes(nodal_disp)
    ref_pad = jnp.pad(ref_image, 1)
    deformed_pad = jnp.pad(deformed_image, ELEM)
    layers = NZ // ELEM
    zero = jnp.zeros((), jnp.int32)

    def layer(index):
        ref_slab = lax.dynamic_slice(ref_pad, (index * ELEM, zero, zero), (ELEM + 2, NY + 2, NX + 2))
        deformed_slab = lax.dynamic_slice(deformed_pad, (index * ELEM, zero, zero), (3 * ELEM, NY + 2 * ELEM, NX + 2 * ELEM))
        node_slab = lax.dynamic_slice(nodes, (zero, index, zero, zero), (3, 2, NY // ELEM + 1, NX // ELEM + 1))
        return element_terms(ref_slab, deformed_slab, node_slab)

    rhs_layers, hess_layers = lax.map(layer, jnp.arange(layers, dtype=jnp.int32))
    rhs = jnp.pad(jnp.moveaxis(rhs_layers[:, :, 0], 0, 1), ((0, 0), (0, 1), (0, 0), (0, 0)))
    rhs = rhs + jnp.pad(jnp.moveaxis(rhs_layers[:, :, 1], 0, 1), ((0, 0), (1, 0), (0, 0), (0, 0)))
    hessian = jnp.moveaxis(hess_layers[..., 0, :, :], 0, 8)

    def operator(field):
        return apply_local(hessian, field) + damping * field

    solution = jnp.zeros_like(rhs)
    residual, direction = rhs, rhs
    norm_now = jnp.sum(residual * residual)
    for step in range(CGSTEPS):
        image = operator(direction)
        alpha = norm_now / jnp.sum(direction * image)
        solution = solution + alpha * direction
        residual = residual - alpha * image
        norm_next = jnp.sum(residual * residual)
        direction = residual + (norm_next / norm_now) * direction
        norm_now = norm_next
    return expand_nodes(float(quantum) * solution), expand_nodes(residual)
```

```python
import jax
import jax.numpy as jnp
import numpy as np
from jax import lax
from jax.experimental import pallas as pl
from jax.experimental.pallas import tpu as pltpu
from jax.sharding import PartitionSpec as P

E = 16
CGSTEPS = 8
QUANTUM = 64
DAMPING = 0.5
BZ, BY, BX = 16, 64, 128
NGZ, NGY, NGX = 4, 8, 4
JY, JX = 5, 9
BLK = JY * JX
HI = lax.Precision.HIGHEST
PAIRS = ((0, 0), (0, 1), (0, 2), (1, 1), (1, 2), (2, 2))
PAIR_OF = {(0, 0): 0, (0, 1): 1, (0, 2): 2, (1, 1): 3, (1, 2): 4, (2, 2): 5}
KROWS = 24
RROWS = 8
F32 = jnp.float32

_T = (np.arange(E) + 0.5) / E
_W0, _W1 = 1.0 - _T, _T


def _place(kinds, count):
    low, high, mixed = kinds
    rows = np.zeros((count + 1 + (count if mixed is not None else 0), count * E), np.float32)
    for e in range(count):
        rows[e, e * E:(e + 1) * E] += low
        rows[e + 1, e * E:(e + 1) * E] += high
        if mixed is not None:
            rows[count + 1 + e, e * E:(e + 1) * E] = mixed
    return rows


def _left(rows, fields):
    out = np.zeros((rows.shape[0] * 8, fields * BY), np.float32)
    for q in range(rows.shape[0]):
        for f in range(fields):
            out[q * 8 + f, f * BY:(f + 1) * BY] = rows[q]
    return out


def _right(rows, scale):
    out = np.zeros((BX, BX), np.float32)
    out[:, :rows.shape[0]] = rows.T * scale
    return out


_SQ = (_W0 * _W0, _W1 * _W1, _W0 * _W1)
_LIN = (_W0, _W1, None)
LEFT_K = _left(_place(_SQ, 4), 6)
RIGHT_K = _right(_place(_SQ, 8), 0.25 / E**2)
LEFT_R = _left(_place(_LIN, 4), 3)
RIGHT_R = _right(_place(_LIN, 8), 0.5 / E**2)


def lanes(shape=(8, BX)):
    return lax.broadcasted_iota(jnp.int32, shape, len(shape) - 1)


def roll(x, amount, axis=1):
    size = x.shape[axis]
    if isinstance(amount, int):
        amount %= size
        if amount == 0:
            return x
    return pltpu.roll(x, amount, axis)


def faces_kernel(ref, z0, z1, y0, y1, x0, x1):
    z0[...] = ref[0:1]
    z1[...] = ref[BZ - 1:BZ]
    for z in range(BZ):
        y0[z:z + 1, :] = ref[z, 0:1, :]
        y1[z:z + 1, :] = ref[z, BY - 1:BY, :]
    lane = lanes((BY, BX))
    first = jnp.zeros((BY, BX), F32)
    last = jnp.zeros((BY, BX), F32)
    for z in range(BZ):
        plane = ref[z]
        first = jnp.where(lane == z, roll(plane, z), first)
        last = jnp.where(lane == z, roll(plane, z + 1), last)
    x0[...] = first
    x1[...] = last


def faces(ref):
    shapes = ((1, BY, BX), (1, BY, BX), (BZ, BX), (BZ, BX), (BY, BX), (BY, BX))
    return pl.pallas_call(
        faces_kernel,
        out_shape=[jax.ShapeDtypeStruct(s, F32) for s in shapes],
        name="faces",
    )(ref)


def fill_padded(pad, ref, zlo, zhi, ylo, yhi):
    pad[1:BZ + 1, 8:8 + BY, :] = ref[...]
    pad[0:1, 8:8 + BY, :] = zlo[...]
    pad[BZ + 1:BZ + 2, 8:8 + BY, :] = zhi[...]
    for z in range(BZ):
        pad[z + 1, 7:8, :] = ylo[z:z + 1, :]
        pad[z + 1, 8 + BY:9 + BY, :] = yhi[z:z + 1, :]


def slopes(pad, xlo, xhi, z, y, lane):
    here = pad[z + 1, pl.ds(8 + y, 8), :]
    along_z = pad[z + 2, pl.ds(8 + y, 8), :] - pad[z, pl.ds(8 + y, 8), :]
    along_y = pad[z + 1, pl.ds(9 + y, 8), :] - pad[z + 1, pl.ds(7 + y, 8), :]
    after = jnp.where(lane == BX - 1, roll(xhi, BX - 1 - z), roll(here, BX - 1))
    before = jnp.where(lane == 0, roll(xlo, -z), roll(here, 1))
    return along_z, along_y, after - before, here


def operator_kernel(ref, zlo, zhi, ylo, yhi, xlo, xhi, left, right, out, pad, acc):
    fill_padded(pad, ref, zlo, zhi, ylo, yhi)
    lane = lanes()

    def rows(step, carry):
        y = pl.multiple_of(step * 8, 8)
        low, high = xlo[pl.ds(y, 8), :], xhi[pl.ds(y, 8), :]
        sums = [[None] * 6 for _ in range(3)]
        for z in range(BZ):
            g = slopes(pad, low, high, z, y, lane)
            for p, (c, d) in enumerate(PAIRS):
                product = g[c] * g[d]
                for k in range(3):
                    term = product * float(_SQ[k][z])
                    sums[k][p] = term if z == 0 else sums[k][p] + term
        for k in range(3):
            for p in range(6):
                acc[k, pl.ds(p * BY + y, 8), :] = sums[k][p]
        return carry

    lax.fori_loop(0, BY // 8, rows, 0)
    packed = [jnp.zeros((8, BX), F32) for _ in range(4)]
    for k in range(3):
        half = jnp.dot(left[...], acc[k], precision=HI, preferred_element_type=F32)
        full = jnp.dot(half, right[...], precision=HI, preferred_element_type=F32)
        kz = 1 if k == 2 else 0
        for q in range(9):
            ky, jy = (0, q) if q < 5 else (1, q - 5)
            piece = full[q * 8:q * 8 + 8]
            for kx in range(2):
                if kz == 0:
                    row, base = ky * 2 + kx, BLK * k
                elif ky == 1:
                    row, base = 1 - kx, 90
                else:
                    row, base = 2 + kx, 81
                source = 0 if kx == 0 else 9
                width = 9 if kx == 0 else 8
                part = jnp.where((lane >= source) & (lane < source + width), piece, 0.0)
                packed[row] = packed[row] + roll(part, base + jy * JX - source)
    for row in range(4):
        out[row * 6:row * 6 + 6, :] = packed[row][0:6]


def operator(ref, halo):
    return pl.pallas_call(
        operator_kernel,
        out_shape=jax.ShapeDtypeStruct((KROWS, BX), F32),
        scratch_shapes=[
            pltpu.VMEM((BZ + 2, BY + 16, BX), F32),
            pltpu.VMEM((3, 6 * BY, BX), F32),
        ],
        name="operator",
    )(ref, *halo, jnp.asarray(LEFT_K), jnp.asarray(RIGHT_K))


PZ, PY = 3 * E, BY + 2 * E
GROUP = PZ // 8


def strips_kernel(mid, zlo, zhi, ylo, yhi, first, last):
    lane = lanes()
    for zz in range(GROUP):
        for tile in range(PY // 8):
            a = jnp.zeros((8, BX), F32)
            b = jnp.zeros((8, BX), F32)
            for g in range(8):
                z = g * GROUP + zz
                if tile < 2:
                    v = ylo[z, tile * 8:tile * 8 + 8, :]
                elif tile >= 10:
                    v = yhi[z, (tile - 10) * 8:(tile - 10) * 8 + 8, :]
                else:
                    source = (zlo, mid, zhi)[z // E]
                    v = source[z % E, (tile - 2) * 8:(tile - 2) * 8 + 8, :]
                mask = (lane >= 16 * g) & (lane < 16 * g + 16)
                a = jnp.where(mask, roll(v, 16 * g), a)
                b = jnp.where(mask, roll(v, 16 * g + 16), b)
            first[zz, tile * 8:tile * 8 + 8, :] = a
            last[zz, tile * 8:tile * 8 + 8, :] = b


def strips(mid, zlo, zhi, ylo, yhi):
    shape = jax.ShapeDtypeStruct((GROUP, PY, BX), F32)
    return pl.pallas_call(strips_kernel, out_shape=[shape, shape], name="strips")(
        mid, zlo, zhi, ylo, yhi
    )


def rhs_kernel(
    summed, ref, zlo, zhi, ylo, yhi, xlo, xhi, left, right,
    dmid, dzlo, dzhi, dylo, dyhi, dxlo, dxhi, out, pad, acc, tiles, warped, sems,
):
    copies = [
        pltpu.make_async_copy(dmid, tiles.at[0, E:2 * E, E:E + BY, :], sems.at[0]),
        pltpu.make_async_copy(dzlo, tiles.at[0, 0:E, E:E + BY, :], sems.at[1]),
        pltpu.make_async_copy(dzhi, tiles.at[0, 2 * E:3 * E, E:E + BY, :], sems.at[2]),
        pltpu.make_async_copy(dylo, tiles.at[0, :, 0:E, :], sems.at[3]),
        pltpu.make_async_copy(dyhi, tiles.at[0, :, E + BY:PY, :], sems.at[4]),
    ]
    for copy in copies:
        copy.start()
    fill_padded(pad, ref, zlo, zhi, ylo, yhi)
    lane = lanes()
    lane96 = lanes((PY, BX))
    for copy in copies:
        copy.wait()

    def widen(zz, carry):
        low, high = dxlo[zz], dxhi[zz]
        for g in range(8):
            z = g * GROUP + zz
            plane = tiles[0, z]
            tiles[1, z] = jnp.where(lane96 >= 112, roll(low, 112 - 16 * g), plane)
            tiles[2, z] = jnp.where(lane96 < 16, roll(high, -16 * g), plane)
        return carry

    lax.fori_loop(0, GROUP, widen, 0)
    lane16 = lanes((E, BX))

    def element(e, carry):
        ey, ex = e // 8, e % 8
        sz, sy, sx = summed[e], summed[32 + e], summed[64 + e]
        whole_z = lax.shift_right_arithmetic(sz, 9)
        whole_y = lax.shift_right_arithmetic(sy, 9)
        whole_x = lax.shift_right_arithmetic(sx, 9)
        scale = 1.0 / (8.0 * QUANTUM)
        fz = (sz & 511).astype(F32) * scale
        fy = (sy & 511).astype(F32) * scale
        fx = (sx & 511).astype(F32) * scale
        which = jnp.where(ex == 0, 1, jnp.where(ex == 7, 2, 0))
        start_z = whole_z + E
        start_y = whole_y + E + ey * E
        turn = jnp.where(whole_x > 0, BX - whole_x, -whole_x)
        mask = (lane16 >= ex * 16) & (lane16 < ex * 16 + 16)
        row = pl.multiple_of(ey * E, E)

        def plane(k):
            a = tiles[which, start_z + k, pl.ds(start_y, E), :]
            b = tiles[which, start_z + k, pl.ds(start_y + 1, E), :]
            return (1.0 - fy) * a + fy * b

        below = plane(0)
        for k in range(E):
            above = plane(k + 1)
            v = (1.0 - fz) * below + fz * above
            v = pltpu.roll(v, turn, 1)
            v = (1.0 - fx) * v + fx * roll(v, BX - 1)
            warped[k, pl.ds(row, E), :] = jnp.where(mask, v, warped[k, pl.ds(row, E), :])
            below = above
        return carry

    lax.fori_loop(0, 32, element, 0)

    def rows(step, carry):
        y = pl.multiple_of(step * 8, 8)
        low, high = xlo[pl.ds(y, 8), :], xhi[pl.ds(y, 8), :]
        sums = [[None] * 3 for _ in range(2)]
        for z in range(BZ):
            *g, here = slopes(pad, low, high, z, y, lane)
            mismatch = here - warped[z, pl.ds(y, 8), :]
            for c in range(3):
                product = g[c] * mismatch
                for k in range(2):
                    term = product * float(_LIN[k][z])
                    sums[k][c] = term if z == 0 else sums[k][c] + term
        for k in range(2):
            for c in range(3):
                acc[k, pl.ds(c * BY + y, 8), :] = sums[k][c]
        return carry

    lax.fori_loop(0, BY // 8, rows, 0)
    packed = jnp.zeros((8, BX), F32)
    for k in range(2):
        half = jnp.dot(left[...], acc[k], precision=HI, preferred_element_type=F32)
        full = jnp.dot(half, right[...], precision=HI, preferred_element_type=F32)
        for jy in range(JY):
            part = jnp.where(lane < JX, full[jy * 8:jy * 8 + 8], 0.0)
            packed = packed + roll(part, BLK * k + jy * JX)
    out[...] = packed


def rhs_terms(summed, ref, halo, dmid, dzlo, dzhi, dylo, dyhi, dxlo, dxhi):
    vmem = pl.BlockSpec(memory_space=pltpu.VMEM)
    anyw = pl.BlockSpec(memory_space=pl.ANY)
    return pl.pallas_call(
        rhs_kernel,
        out_shape=jax.ShapeDtypeStruct((RROWS, BX), F32),
        in_specs=[pl.BlockSpec(memory_space=pltpu.SMEM)] + [vmem] * 9 + [anyw] * 5 + [vmem] * 2,
        out_specs=vmem,
        scratch_shapes=[
            pltpu.VMEM((BZ + 2, BY + 16, BX), F32),
            pltpu.VMEM((2, 3 * BY, BX), F32),
            pltpu.VMEM((3, PZ, PY, BX), F32),
            pltpu.VMEM((BZ, BY, BX), F32),
            pltpu.SemaphoreType.DMA((5,)),
        ],
        name="rhs",
    )(summed, ref, *halo, jnp.asarray(LEFT_R), jnp.asarray(RIGHT_R),
      dmid, dzlo, dzhi, dylo, dyhi, dxlo, dxhi)


NZ = NGZ + 1
TILES = NZ * 2


def cg_kernel(where, *refs):
    kparts, rparts = refs[:NGY], refs[NGY:2 * NGY]
    out_x, out_r = refs[2 * NGY:2 * NGY + 2]
    kbuf, rbuf, stencil, shifted, xs, rs, ys, sems = refs[2 * NGY + 2:]
    kn, rn = NGZ * NGX * KROWS, NGZ * NGX * RROWS
    copies = []
    for i in range(NGY):
        copies.append(
            pltpu.make_async_copy(kparts[i], kbuf.at[i * kn:(i + 1) * kn, :], sems.at[i]))
        copies.append(
            pltpu.make_async_copy(rparts[i], rbuf.at[i * rn:(i + 1) * rn, :], sems.at[NGY + i]))
    for copy in copies:
        copy.start()
    for copy in copies:
        copy.wait()
    own_z, own_y, own_x = where[0], where[1], where[2]
    lane = lanes()
    sub = lax.broadcasted_iota(jnp.int32, (8, BX), 0)

    def brick(buf, rows, gz, gx, row):
        rel = ((gx - own_x) & 3) * 4 + ((gz - own_z) & 3)
        v = buf[pl.ds(rel * rows + row, 8, stride=16 * rows), :]
        return pltpu.roll(v, own_y, 0)

    even, odd = lane < BLK, (lane >= BLK) & (lane < 2 * BLK)
    zero = jnp.zeros((8, BX), F32)

    def planes(s, width):
        out = []
        even_w = lane < width
        odd_w = (lane >= BLK) & (lane < BLK + width)
        for z in range(NZ):
            for h in range(2):
                e, o = zero, zero
                if z < NGZ:
                    e = s[z][2 * h]
                    o = roll(s[z][2 * h + 1], BLK)
                if z > 0:
                    e = e + roll(s[z - 1][2 * h], -BLK)
                    o = o + s[z - 1][2 * h + 1]
                out.append(jnp.where(even_w, e, jnp.where(odd_w, o, zero)))
        return out

    def edges(s, base, width):
        out = []
        even_w = lane < width
        odd_w = (lane >= BLK) & (lane < BLK + width)
        for z in range(NGZ):
            for h in range(2):
                e = roll(s[z][2 * h], -base)
                o = roll(s[z][2 * h + 1], BLK - base)
                out.append(jnp.where(even_w, e, jnp.where(odd_w, o, zero)))
        return out

    def build(pair, carry):
        for row in range(4):
            s = [[brick(kbuf, KROWS, gz, gx, row * 6 + pair) for gx in range(NGX)]
                 for gz in range(NGZ)]
            upper = (1, 1, 0, 0)[row]
            sides = (
                (0, row >> 1, row & 1, planes(s, 36 if row >> 1 else BLK)),
                (1, upper, (1, 0, 0, 1)[row],
                 edges(s, 90 if upper else 81, 36 if upper else BLK)),
            )
            for kz, ky, kx, field in sides:
                for oy in ((0,) if ky == 0 else (1, -1)):
                    for ox in ((0,) if kx == 0 else (1, -1)):
                        amount = (JX if oy == -1 else 0) + (1 if ox == 1 else 0)
                        slot = (kz * 3 + oy + 1) * 3 + ox + 1
                        for i, v in enumerate(field):
                            stencil[slot, pair, i] = roll(v, amount)
        return carry

    lax.fori_loop(0, 6, build, 0)

    def fold(c, z, y0, y1):
        a = y0 + jnp.where(m_odd0, roll(y0, 37), 0.0) + jnp.where(m_even8, roll(y0, -37), 0.0)
        b = y1 + jnp.where(m_odd0, roll(y1, 37), 0.0) + jnp.where(m_even8, roll(y1, -37), 0.0)
        a = a + jnp.where(m_odd8, roll(y1, 53), 0.0)
        b = b + jnp.where(m_even0, roll(y0, -53), 0.0)
        out = []
        for v in (a, b):
            up = roll(roll(v, 36), 7, 0)
            down = roll(roll(v, -36), 1, 0)
            out.append(v + jnp.where(m_top, up, 0.0) + jnp.where(m_bottom, down, 0.0))
        return out

    inside = lax.rem(lane, BLK)
    jy = inside // JX
    jx = lax.rem(inside, JX)
    m_odd0, m_odd8 = odd & (jx == 0), odd & (jx == 8)
    m_even0, m_even8 = even & (jx == 0), even & (jx == 8)
    valid = lane < 2 * BLK
    m_top = valid & (jy == 4) & (sub < 7)
    m_bottom = valid & (jy == 0) & (sub > 0)
    base = valid & ((jy < 4) | (sub == 7))
    owner = (
        jnp.where(base & (jx < 8), 1.0, 0.0),
        jnp.where(base & ((jx < 8) | odd), 1.0, 0.0),
    )

    def total(v):
        return jnp.sum(jnp.sum(v, axis=1, keepdims=True), axis=0, keepdims=True)

    part = [zero, zero]
    for c in range(3):
        s = [[brick(rbuf, RROWS, gz, gx, c) for gx in range(NGX)] for gz in range(NGZ)]
        field = planes(s, BLK)
        for z in range(NZ):
            pair_ = fold(c, z, field[2 * z], field[2 * z + 1])
            for h in range(2):
                v = pair_[h]
                i = 2 * z + h
                rs[c, i] = v
                xs[c, i] = zero
                shifted[c, 1, i] = v
                shifted[c, 0, i] = roll(v, JX)
                shifted[c, 2, i] = roll(v, -JX)
                part[h] = part[h] + v * v
    norm = total(part[0] * owner[0] + part[1] * owner[1])

    def step(_, norm_now):
        part = [zero, zero]
        for z in range(NZ):
            for h in range(2):
                sums = [[None] * 3 for _ in range(3)]
                for oz in (-1, 0, 1):
                    if not 0 <= z + oz < NZ:
                        continue
                    kz = 0 if oz == 0 else 1
                    kt = (z - 1 if oz == -1 else z) * 2 + h
                    for oy in range(3):
                        p = [shifted[d, oy, (z + oz) * 2 + h] for d in range(3)]
                        for ox in range(3):
                            slot = (kz * 3 + oy) * 3 + ox
                            k = [stencil[slot, q, kt] for q in range(6)]
                            for c in range(3):
                                for d in range(3):
                                    term = k[PAIR_OF[min(c, d), max(c, d)]] * p[d]
                                    old = sums[c][ox]
                                    sums[c][ox] = term if old is None else old + term
                for c in range(3):
                    ys[c, 2 * z + h] = sums[c][1] + roll(sums[c][0], 1) + roll(sums[c][2], -1)
            for c in range(3):
                pair_ = fold(c, z, ys[c, 2 * z], ys[c, 2 * z + 1])
                for h in range(2):
                    i = 2 * z + h
                    p = shifted[c, 1, i]
                    v = pair_[h] + DAMPING * p
                    ys[c, i] = v
                    part[h] = part[h] + v * p
        alpha = norm_now / total(part[0] * owner[0] + part[1] * owner[1])
        part = [zero, zero]
        for c in range(3):
            for i in range(TILES):
                xs[c, i] = xs[c, i] + alpha * shifted[c, 1, i]
                r = rs[c, i] - alpha * ys[c, i]
                rs[c, i] = r
                part[i % 2] = part[i % 2] + r * r
        norm_next = total(part[0] * owner[0] + part[1] * owner[1])
        beta = norm_next / norm_now
        for c in range(3):
            for i in range(TILES):
                p = rs[c, i] + beta * shifted[c, 1, i]
                shifted[c, 1, i] = p
                shifted[c, 0, i] = roll(p, JX)
                shifted[c, 2, i] = roll(p, -JX)
        return norm_next

    lax.fori_loop(0, CGSTEPS, step, norm)

    half, side = own_x >> 1, own_x & 1
    turn = jnp.where(side == 1, BX - BLK, 0)
    for src, dst, scale in ((xs, out_x, float(QUANTUM)), (rs, out_r, 1.0)):
        for c in range(3):
            for jz in range(2):
                v = src[c, (own_z + jz) * 2 + half]
                v = pltpu.roll(pltpu.roll(v, turn, 1), (8 - own_y) & 7, 0) * scale
                tile = zero
                for j in range(JY):
                    row = roll(roll(v, -j * JX), j, 0)
                    tile = jnp.where(sub == j, row, tile)
                dst[c, jz] = tile[0:JY, 0:JX]


def solve(where, kparts, rparts):
    anyw = pl.BlockSpec(memory_space=pl.ANY)
    vmem = pl.BlockSpec(memory_space=pltpu.VMEM)
    shape = jax.ShapeDtypeStruct((3, 2, JY, JX), F32)
    field = pltpu.VMEM((3, TILES, 8, BX), F32)
    return pl.pallas_call(
        cg_kernel,
        out_shape=[shape, shape],
        in_specs=[pl.BlockSpec(memory_space=pltpu.SMEM)] + [anyw] * (2 * NGY),
        out_specs=[vmem, vmem],
        scratch_shapes=[
            pltpu.VMEM((NGZ * NGX * NGY * KROWS, BX), F32),
            pltpu.VMEM((NGZ * NGX * NGY * RROWS, BX), F32),
            pltpu.VMEM((18, 6, TILES, 8, BX), F32),
            pltpu.VMEM((3, 3, TILES, 8, BX), F32),
            field, field, field,
            pltpu.SemaphoreType.DMA((2 * NGY,)),
        ],
        name="cg",
    )(where, *kparts, *rparts)


def from_low(x, axis):
    n = lax.axis_size(axis)
    return lax.ppermute(x, axis, [(i, i + 1) for i in range(n - 1)])


def from_high(x, axis):
    n = lax.axis_size(axis)
    return lax.ppermute(x, axis, [(i + 1, i) for i in range(n - 1)])


def ahead(x, axis, s):
    n = lax.axis_size(axis)
    return lax.ppermute(x, axis, [((k + s) % n, k) for k in range(n)])


def gather(x, name):
    with jax.named_scope(name + "_z"):
        x = jnp.concatenate([x] + [ahead(x, "gz", s) for s in range(1, NGZ)], 0)
    with jax.named_scope(name + "_x"):
        x = jnp.concatenate([x] + [ahead(x, "gx", s) for s in range(1, NGX)], 0)
    with jax.named_scope(name + "_y"):
        return [x] + [ahead(x, "gy", s) for s in range(1, NGY)]


def element_sums(nodes):
    low = nodes[:, 0] + nodes[:, 1]
    low = low[:, :-1] + low[:, 1:]
    low = low[:, :, :-1] + low[:, :, 1:]
    return low.reshape(96)


def per_device(ref_image, deformed_image, nodal_disp):
    z0, z1, y0, y1, x0, x1 = faces(ref_image)
    dzlo, dzhi = from_low(deformed_image, "gz"), from_high(deformed_image, "gz")
    halo = (
        from_low(z1, "gz"), from_high(z0, "gz"),
        from_low(y1, "gy"), from_high(y0, "gy"),
        from_low(x1, "gx"), from_high(x0, "gx"),
    )
    summed = element_sums(nodal_disp)
    where = jnp.stack([lax.axis_index("gz"), lax.axis_index("gy"), lax.axis_index("gx")])
    kparts = gather(operator(ref_image, halo), "gk")
    dylo = from_low(
        jnp.concatenate([v[:, BY - E:, :] for v in (dzlo, deformed_image, dzhi)], 0), "gy")
    dyhi = from_high(
        jnp.concatenate([v[:, :E, :] for v in (dzlo, deformed_image, dzhi)], 0), "gy")
    first, last = strips(deformed_image, dzlo, dzhi, dylo, dyhi)
    dxlo, dxhi = from_low(last, "gx"), from_high(first, "gx")
    terms = rhs_terms(
        summed, ref_image, halo, deformed_image, dzlo, dzhi, dylo, dyhi, dxlo, dxhi)
    rparts = gather(terms, "gr")
    return tuple(solve(where, kparts, rparts))


def solution(mesh):
    spec3 = P("gz", "gy", "gx")
    spec4 = P(None, "gz", "gy", "gx")
    return jax.shard_map(
        per_device, mesh=mesh, in_specs=(spec3, spec3, spec4), out_specs=(spec4, spec4),
        check_vma=False,
    )
```

```python
import jax
import jax.numpy as jnp
import numpy as np
from jax import lax
from jax.experimental import pallas as pl
from jax.experimental.pallas import tpu as pltpu
from jax.sharding import PartitionSpec as P

E = 16
CGSTEPS = 8
QUANTUM = 64
DAMPING = 0.5
BZ, BY, BX = 16, 64, 128
NGZ, NGY, NGX = 4, 8, 4
JY, JX = 5, 9
BLK = JY * JX
HI = lax.Precision.HIGHEST
PAIRS = ((0, 0), (0, 1), (0, 2), (1, 1), (1, 2), (2, 2))
PAIR_OF = {(0, 0): 0, (0, 1): 1, (0, 2): 2, (1, 1): 3, (1, 2): 4, (2, 2): 5}
KROWS = 24
RROWS = 4
F32 = jnp.float32

_T = (np.arange(E) + 0.5) / E
_W0, _W1 = 1.0 - _T, _T


def _place(kinds, count):
    low, high, mixed = kinds
    rows = np.zeros((count + 1 + (count if mixed is not None else 0), count * E), np.float32)
    for e in range(count):
        rows[e, e * E:(e + 1) * E] += low
        rows[e + 1, e * E:(e + 1) * E] += high
        if mixed is not None:
            rows[count + 1 + e, e * E:(e + 1) * E] = mixed
    return rows


def _left(rows, fields):
    out = np.zeros((rows.shape[0] * 8, fields * BY), np.float32)
    for q in range(rows.shape[0]):
        for f in range(fields):
            out[q * 8 + f, f * BY:(f + 1) * BY] = rows[q]
    return out


def _right(rows, scale):
    out = np.zeros((BX, BX), np.float32)
    out[:, :rows.shape[0]] = rows.T * scale
    return out


_SQ = (_W0 * _W0, _W1 * _W1, _W0 * _W1)
_LIN = (_W0, _W1, None)
LEFT_K = _left(_place(_SQ, 4), 6)
RIGHT_K = _right(_place(_SQ, 8), 0.25 / E**2)
LEFT_R = _left(_place(_LIN, 4), 3)
RIGHT_R = _right(_place(_LIN, 8), 0.5 / E**2)


def lanes(shape=(8, BX)):
    return lax.broadcasted_iota(jnp.int32, shape, len(shape) - 1)


def roll(x, amount, axis=1):
    size = x.shape[axis]
    if isinstance(amount, int):
        amount %= size
        if amount == 0:
            return x
    return pltpu.roll(x, amount, axis)


VMEM = pl.BlockSpec(memory_space=pltpu.VMEM)
SMEM = pl.BlockSpec(memory_space=pltpu.SMEM)


def grant(mib):
    return pltpu.CompilerParams(vmem_limit_bytes=mib << 20)


PZ, PY = 3 * E, BY + 2 * E
GROUP = PZ // 8
STRIP = GROUP * PY + BY


def piece(blocks, z, tile):
    mid, zlo, zhi, ylo, yhi = blocks
    if tile < 2:
        return ylo[z, tile * 8:tile * 8 + 8, :]
    if tile >= 10:
        return yhi[z, (tile - 10) * 8:(tile - 10) * 8 + 8, :]
    return (zlo, mid, zhi)[z // E][z % E, (tile - 2) * 8:(tile - 2) * 8 + 8, :]


def strips_kernel(ref, mid, zlo, zhi, ylo, yhi, first, last):
    blocks = (mid, zlo, zhi, ylo, yhi)
    lane = lanes()
    for zz in range(GROUP):
        for tile in range(PY // 8):
            a = jnp.zeros((8, BX), F32)
            b = jnp.zeros((8, BX), F32)
            for g in range(8):
                v = piece(blocks, g * GROUP + zz, tile)
                mask = (lane >= 16 * g) & (lane < 16 * g + 16)
                a = jnp.where(mask, roll(v, 16 * g), a)
                b = jnp.where(mask, roll(v, 16 * g + 16), b)
            row = zz * PY + tile * 8
            first[row:row + 8, :] = a
            last[row:row + 8, :] = b
    for tile in range(BY // 8):
        a = jnp.zeros((8, BX), F32)
        b = jnp.zeros((8, BX), F32)
        for z in range(BZ):
            v = ref[z, tile * 8:tile * 8 + 8, :]
            a = jnp.where(lane == z, roll(v, z), a)
            b = jnp.where(lane == z, roll(v, z + 1), b)
        row = GROUP * PY + tile * 8
        first[row:row + 8, :] = a
        last[row:row + 8, :] = b


def strips(ref, *blocks):
    shape = jax.ShapeDtypeStruct((STRIP, BX), F32)
    return pl.pallas_call(
        strips_kernel,
        out_shape=[shape, shape],
        in_specs=[VMEM] * 6,
        out_specs=[VMEM] * 2,
        compiler_params=grant(8),
        name="strips",
    )(ref, *blocks)


def warp_element(summed, tile, ey, ex, warped):
    lane = lanes((E, BX))
    e = ey * 8 + ex
    sz, sy, sx = summed[e], summed[32 + e], summed[64 + e]
    whole_z = lax.shift_right_arithmetic(sz, 9)
    whole_y = lax.shift_right_arithmetic(sy, 9)
    whole_x = lax.shift_right_arithmetic(sx, 9)
    scale = 1.0 / (8.0 * QUANTUM)
    fz = (sz & 511).astype(F32) * scale
    fy = (sy & 511).astype(F32) * scale
    fx = (sx & 511).astype(F32) * scale
    start_z = whole_z + E
    start_y = whole_y + E + ey * E
    turn = jnp.where(whole_x > 0, BX - whole_x, -whole_x)
    mask = (lane >= ex * 16) & (lane < ex * 16 + 16)
    row = pl.multiple_of(ey * E, E)

    def plane(k):
        a = tile[start_z + k, pl.ds(start_y, E), :]
        b = tile[start_z + k, pl.ds(start_y + 1, E), :]
        return (1.0 - fy) * a + fy * b

    below = plane(0)
    for k in range(E):
        above = plane(k + 1)
        v = (1.0 - fz) * below + fz * above
        v = pltpu.roll(v, turn, 1)
        v = (1.0 - fx) * v + fx * roll(v, BX - 1)
        pltpu.store(warped.at[k, pl.ds(row, E), :], v, mask=mask)
        below = above


def inner_kernel(summed, mid, zlo, zhi, ylo, yhi, warped, tile):
    blocks = (mid, zlo, zhi, ylo, yhi)
    for z in range(PZ):
        for t in range(PY // 8):
            tile[z, t * 8:t * 8 + 8, :] = piece(blocks, z, t)

    def pair(i, carry):
        for ex in range(2):
            warp_element(summed, tile, i // 3, 1 + 2 * (i % 3) + ex, warped)
        return carry

    lax.fori_loop(0, 12, pair, 0)


def inner(summed, *blocks):
    return pl.pallas_call(
        inner_kernel,
        out_shape=jax.ShapeDtypeStruct((BZ, BY, BX), F32),
        in_specs=[SMEM] + [VMEM] * 5,
        out_specs=VMEM,
        scratch_shapes=[pltpu.VMEM((PZ, PY, BX), F32)],
        compiler_params=grant(10),
        name="inner",
    )(summed, *blocks)


def slopes(pad, xlo, xhi, z, y, lane):
    here = pad[z + 1, pl.ds(8 + y, 8), :]
    along_z = pad[z + 2, pl.ds(8 + y, 8), :] - pad[z, pl.ds(8 + y, 8), :]
    along_y = pad[z + 1, pl.ds(9 + y, 8), :] - pad[z + 1, pl.ds(7 + y, 8), :]
    after_ = jnp.where(lane == BX - 1, roll(xhi, BX - 1 - z), roll(here, BX - 1))
    before = jnp.where(lane == 0, roll(xlo, -z), roll(here, 1))
    return (along_z, along_y, after_ - before), here


def terms_kernel(
    summed, ref, rzlo, rzhi, mid, zlo, zhi, ylo, yhi, xlo, xhi, inside,
    left_k, right_k, left_r, right_r, out, pad, tiles, warped, acc_k, acc_r,
):
    blocks = (mid, zlo, zhi, ylo, yhi)
    lane = lanes()
    pad[1:BZ + 1, 8:8 + BY, :] = ref[...]
    pad[0:1, 8:8 + BY, :] = rzlo[...]
    pad[BZ + 1:BZ + 2, 8:8 + BY, :] = rzhi[...]
    for z in range(BZ):
        pad[z + 1, 7:8, :] = ylo[PZ, z:z + 1, :]
        pad[z + 1, 8 + BY:9 + BY, :] = yhi[PZ, z:z + 1, :]
    for z in range(PZ):
        g, zz = z // GROUP, z % GROUP
        for t in range(PY // 8):
            v = piece(blocks, z, t)
            row = zz * PY + t * 8
            low, high = xlo[row:row + 8, :], xhi[row:row + 8, :]
            tiles[0, z, t * 8:t * 8 + 8, :] = jnp.where(lane >= 112, roll(low, 112 - 16 * g), v)
            tiles[1, z, t * 8:t * 8 + 8, :] = jnp.where(lane < 16, roll(high, -16 * g), v)

    def element(ey, carry):
        warp_element(summed, tiles.at[0], ey, 0, warped)
        warp_element(summed, tiles.at[1], ey, 7, warped)
        return carry

    lax.fori_loop(0, 4, element, 0)
    middle = (lane >= 16) & (lane < 112)

    def rows(step, carry):
        y = pl.multiple_of(step * 8, 8)
        face = pl.multiple_of(GROUP * PY + y, 8)
        low, high = xlo[pl.ds(face, 8), :], xhi[pl.ds(face, 8), :]
        sums = [[None] * 6 for _ in range(3)]
        sums_r = [[None] * 3 for _ in range(2)]

        def add(where, k, i, term):
            where[k][i] = term if where[k][i] is None else where[k][i] + term

        for z in range(BZ):
            g, here = slopes(pad, low, high, z, y, lane)
            for p, (c, d) in enumerate(PAIRS):
                product = g[c] * g[d]
                for k in range(3):
                    add(sums, k, p, product * float(_SQ[k][z]))
            moved = jnp.where(middle, inside[z, pl.ds(y, 8), :], warped[z, pl.ds(y, 8), :])
            mismatch = here - moved
            for c in range(3):
                product = g[c] * mismatch
                for k in range(2):
                    add(sums_r, k, c, product * float(_LIN[k][z]))
        for k in range(3):
            for p in range(6):
                acc_k[k, pl.ds(p * BY + y, 8), :] = sums[k][p]
        for k in range(2):
            for c in range(3):
                acc_r[k, pl.ds(c * BY + y, 8), :] = sums_r[k][c]
        return carry

    lax.fori_loop(0, BY // 8, rows, 0)

    def contract(left, fields, right):
        half = jnp.dot(left[...], fields, precision=HI, preferred_element_type=F32)
        return jnp.dot(half, right[...], precision=HI, preferred_element_type=F32)

    packed = [jnp.zeros((8, BX), F32) for _ in range(5)]
    for k in range(3):
        full = contract(left_k, acc_k[k], right_k)
        kz = 1 if k == 2 else 0
        for q in range(9):
            ky, jy = (0, q) if q < 5 else (1, q - 5)
            rows_ = full[q * 8:q * 8 + 8]
            for kx in range(2):
                if kz == 0:
                    row, base = ky * 2 + kx, BLK * k
                elif ky == 1:
                    row, base = 1 - kx, 90
                else:
                    row, base = 2 + kx, 81
                source = 0 if kx == 0 else 9
                width = 9 if kx == 0 else 8
                part = jnp.where((lane >= source) & (lane < source + width), rows_, 0.0)
                packed[row] = packed[row] + roll(part, base + jy * JX - source)
    for k in range(2):
        full = contract(left_r, acc_r[k], right_r)
        for jy in range(JY):
            part = jnp.where(lane < JX, full[jy * 8:jy * 8 + 8], 0.0)
            packed[4] = packed[4] + roll(part, BLK * k + jy * JX)
    for row in range(4):
        out[row * 6:row * 6 + 6, :] = packed[row][0:6]
    out[KROWS:KROWS + 8, :] = packed[4]


def terms(summed, *arrays):
    return pl.pallas_call(
        terms_kernel,
        out_shape=jax.ShapeDtypeStruct((KROWS + 8, BX), F32),
        in_specs=[SMEM] + [VMEM] * 15,
        out_specs=VMEM,
        scratch_shapes=[
            pltpu.VMEM((BZ + 2, BY + 16, BX), F32),
            pltpu.VMEM((2, PZ, PY, BX), F32),
            pltpu.VMEM((BZ, BY, BX), F32),
            pltpu.VMEM((3, 6 * BY, BX), F32),
            pltpu.VMEM((2, 3 * BY, BX), F32),
        ],
        compiler_params=grant(20),
        name="terms",
    )(summed, *arrays, jnp.asarray(LEFT_K), jnp.asarray(RIGHT_K),
      jnp.asarray(LEFT_R), jnp.asarray(RIGHT_R))


NZ = NGZ + 1
TILES = NZ * 2


SLOTS0 = 54 * TILES
SLOTS = SLOTS0 + 54 * 2 * NGZ


STEPS = (("gz", 2, 0), ("gx", 2, 0), ("gy", 4, 0), ("gz", 1, 0), ("gy", 2, 1), ("gx", 1, 1))
SIZE = {"gz": NGZ, "gx": NGX, "gy": NGY}
PAIR = 2 * (KROWS + RROWS)


def units():
    def moved(held, axis, s):
        return [dict(u, **{axis: (u[axis] + s) % SIZE[axis]}) for u in held]

    held = [{"gz": 0, "gx": 0, "gy": 0}]
    for axis, s, both in STEPS[1:]:
        n = len(held) // 2
        if both:
            held = held + moved(held[:n], axis, s) + moved(held[n:], axis, -s)
        else:
            held = held + moved(held, axis, s)
    assert len({tuple(u.values()) for u in held}) == len(held) == 32
    assert all(u["gz"] < 2 and u["gy"] % 2 == 0 for u in held)
    return held


def runs():
    out = []
    for i, u in enumerate(units()):
        place, dy = relative(u["gz"], u["gx"]) // 2, u["gy"]
        if out and out[-1][1] + out[-1][2] == place and out[-1][3] == dy:
            out[-1][2] += 1
        else:
            out.append([i, place, 1, dy])
    return out


def relative(dz, dx):
    return ((dx & 1) * 2 + (dz & 1)) * 4 + (dx >> 1) * 2 + (dz >> 1)


def brick(buf, where, gz, gx, row, rhs):
    rel = relative((gz - where[0]) & 3, (gx - where[2]) & 3)
    inner_row = 2 * KROWS + (rel & 1) * RROWS if rhs else (rel & 1) * KROWS
    return buf[(rel >> 1) * PAIR + inner_row + row]


def stencil_slot(kz, oy, ox, pair, i):
    slot = ((oy + 1) * 3 + ox + 1) * 6 + pair
    return slot * TILES + i if kz == 0 else SLOTS0 + slot * 2 * NGZ + i


def planes(s, width):
    lane = lanes()
    zero = jnp.zeros((8, BX), F32)
    out = []
    for z in range(NZ):
        for h in range(2):
            e, o = zero, zero
            if z < NGZ:
                e = s[z][2 * h]
                o = roll(s[z][2 * h + 1], BLK)
            if z > 0:
                e = e + roll(s[z - 1][2 * h], -BLK)
                o = o + s[z - 1][2 * h + 1]
            odd = (lane >= BLK) & (lane < BLK + width)
            out.append(jnp.where(lane < width, e, jnp.where(odd, o, zero)))
    return out


def edges(s, base, width):
    lane = lanes()
    out = []
    for z in range(NGZ):
        for h in range(2):
            e = roll(s[z][2 * h], -base)
            o = roll(s[z][2 * h + 1], BLK - base)
            odd = (lane >= BLK) & (lane < BLK + width)
            out.append(jnp.where(lane < width, e, jnp.where(odd, o, 0.0)))
    return out


def cg_kernel(
    where, part0, part1, out_x, out_r, buf, stencil, shifted, xs, rs, ys, sems,
):
    own_z, own_y, own_x = where[0], where[1], where[2]
    copies = []
    for side, part in enumerate((part0, part1)):
        for first, place, count, dy in runs():
            gy = ((own_y ^ side) + dy) & 7
            copies.append(pltpu.make_async_copy(
                part.at[first * PAIR:(first + count) * PAIR, :],
                buf.at[place * PAIR:(place + count) * PAIR, gy, :],
                sems.at[len(copies)]))
    for copy in copies:
        copy.start()
    for copy in copies:
        copy.wait()

    def build(pair, carry):
        for row in range(4):
            s = [[brick(buf, where, gz, gx, row * 6 + pair, False) for gx in range(NGX)]
                 for gz in range(NGZ)]
            upper = (1, 1, 0, 0)[row]
            sides = (
                (0, row >> 1, row & 1, planes(s, 36 if row >> 1 else BLK)),
                (1, upper, (1, 0, 0, 1)[row],
                 edges(s, 90 if upper else 81, 36 if upper else BLK)),
            )
            for kz, ky, kx, field in sides:
                for oy in ((0,) if ky == 0 else (1, -1)):
                    for ox in ((0,) if kx == 0 else (1, -1)):
                        amount = (JX if oy == -1 else 0) + (1 if ox == 1 else 0)
                        for i, v in enumerate(field):
                            stencil[stencil_slot(kz, oy, ox, pair, i)] = roll(v, amount)
        return carry

    lax.fori_loop(0, 6, build, 0)
    lane = lanes()
    sub = lax.broadcasted_iota(jnp.int32, (8, BX), 0)
    even, odd = lane < BLK, (lane >= BLK) & (lane < 2 * BLK)
    zero = jnp.zeros((8, BX), F32)

    def fold(c, z, y0, y1):
        a = y0 + jnp.where(m_odd0, roll(y0, 37), 0.0) + jnp.where(m_even8, roll(y0, -37), 0.0)
        b = y1 + jnp.where(m_odd0, roll(y1, 37), 0.0) + jnp.where(m_even8, roll(y1, -37), 0.0)
        a = a + jnp.where(m_odd8, roll(y1, 53), 0.0)
        b = b + jnp.where(m_even0, roll(y0, -53), 0.0)
        out = []
        for v in (a, b):
            up = roll(roll(v, 36), 7, 0)
            down = roll(roll(v, -36), 1, 0)
            out.append(v + jnp.where(m_top, up, 0.0) + jnp.where(m_bottom, down, 0.0))
        return out

    inside = lax.rem(lane, BLK)
    jy = inside // JX
    jx = lax.rem(inside, JX)
    m_odd0, m_odd8 = odd & (jx == 0), odd & (jx == 8)
    m_even0, m_even8 = even & (jx == 0), even & (jx == 8)
    valid = lane < 2 * BLK
    m_top = valid & (jy == 4) & (sub < 7)
    m_bottom = valid & (jy == 0) & (sub > 0)
    base = valid & ((jy < 4) | (sub == 7))
    owner = (
        jnp.where(base & (jx < 8), 1.0, 0.0),
        jnp.where(base & ((jx < 8) | odd), 1.0, 0.0),
    )

    def total(v):
        return jnp.sum(jnp.sum(v, axis=1, keepdims=True), axis=0, keepdims=True)

    part = [zero, zero]
    for c in range(3):
        s = [[brick(buf, where, gz, gx, c, True) for gx in range(NGX)] for gz in range(NGZ)]
        field = planes(s, BLK)
        for z in range(NZ):
            pair_ = fold(c, z, field[2 * z], field[2 * z + 1])
            for h in range(2):
                v = pair_[h]
                i = 2 * z + h
                rs[c, i] = v
                xs[c, i] = zero
                shifted[c, 1, i] = v
                shifted[c, 0, i] = roll(v, JX)
                shifted[c, 2, i] = roll(v, -JX)
                part[h] = part[h] + v * v
    norm = total(part[0] * owner[0] + part[1] * owner[1])

    def step(_, norm_now):
        part = [zero, zero]
        for z in range(NZ):
            for h in range(2):
                sums = [[None] * 3 for _ in range(3)]
                for oz in (-1, 0, 1):
                    if not 0 <= z + oz < NZ:
                        continue
                    kz = 0 if oz == 0 else 1
                    kt = (z - 1 if oz == -1 else z) * 2 + h
                    for oy in range(3):
                        p = [shifted[d, oy, (z + oz) * 2 + h] for d in range(3)]
                        for ox in range(3):
                            k = [stencil[stencil_slot(kz, oy - 1, ox - 1, q, kt)] for q in range(6)]
                            for c in range(3):
                                for d in range(3):
                                    term = k[PAIR_OF[min(c, d), max(c, d)]] * p[d]
                                    old = sums[c][ox]
                                    sums[c][ox] = term if old is None else old + term
                for c in range(3):
                    ys[c, 2 * z + h] = sums[c][1] + roll(sums[c][0], 1) + roll(sums[c][2], -1)
            for c in range(3):
                pair_ = fold(c, z, ys[c, 2 * z], ys[c, 2 * z + 1])
                for h in range(2):
                    i = 2 * z + h
                    p = shifted[c, 1, i]
                    v = pair_[h] + DAMPING * p
                    ys[c, i] = v
                    part[h] = part[h] + v * p
        alpha = norm_now / total(part[0] * owner[0] + part[1] * owner[1])
        part = [zero, zero]
        for c in range(3):
            for i in range(TILES):
                xs[c, i] = xs[c, i] + alpha * shifted[c, 1, i]
                r = rs[c, i] - alpha * ys[c, i]
                rs[c, i] = r
                part[i % 2] = part[i % 2] + r * r
        norm_next = total(part[0] * owner[0] + part[1] * owner[1])
        beta = norm_next / norm_now
        for c in range(3):
            for i in range(TILES):
                p = rs[c, i] + beta * shifted[c, 1, i]
                shifted[c, 1, i] = p
                shifted[c, 0, i] = roll(p, JX)
                shifted[c, 2, i] = roll(p, -JX)
        return norm_next

    lax.fori_loop(0, CGSTEPS, step, norm)

    half, side = own_x >> 1, own_x & 1
    turn = jnp.where(side == 1, BX - BLK, 0)
    for src, dst, scale in ((xs, out_x, float(QUANTUM)), (rs, out_r, 1.0)):
        for c in range(3):
            for jz in range(2):
                v = src[c, (own_z + jz) * 2 + half]
                v = pltpu.roll(pltpu.roll(v, turn, 1), (8 - own_y) & 7, 0) * scale
                tile = zero
                for j in range(JY):
                    row = roll(roll(v, -j * JX), j, 0)
                    tile = jnp.where(sub == j, row, tile)
                dst[c, jz] = tile[0:JY, 0:JX]


def solve(where, parts):
    shape = jax.ShapeDtypeStruct((3, 2, JY, JX), F32)
    field = pltpu.VMEM((3, TILES, 8, BX), F32)
    return pl.pallas_call(
        cg_kernel,
        out_shape=[shape, shape],
        in_specs=[SMEM] + [VMEM] * 2,
        out_specs=[VMEM, VMEM],
        scratch_shapes=[
            pltpu.VMEM((NGZ * NGX // 2 * PAIR, 8, BX), F32),
            pltpu.VMEM((SLOTS, 8, BX), F32),
            pltpu.VMEM((3, 3, TILES, 8, BX), F32),
            field, field, field,
            pltpu.SemaphoreType.DMA((2 * len(runs()),)),
        ],
        compiler_params=grant(20),
        name="cg",
    )(where, *parts)


def from_low(x, axis):
    n = lax.axis_size(axis)
    return lax.ppermute(x, axis, [(i, i + 1) for i in range(n - 1)])


def from_high(x, axis):
    n = lax.axis_size(axis)
    return lax.ppermute(x, axis, [(i + 1, i) for i in range(n - 1)])


def ahead(x, axis, s):
    n = lax.axis_size(axis)
    return lax.ppermute(x, axis, [((k + s) % n, k) for k in range(n)])


def gather(rows):
    for i, (axis, s, both) in enumerate(STEPS):
        with jax.named_scope("gather_" + axis + str(s)):
            if both:
                n = rows.shape[0] // 2
                theirs = (ahead(rows[:n], axis, s), ahead(rows[n:], axis, -s))
            else:
                theirs = (ahead(rows, axis, s),)
            if i == 0:
                other, = theirs
                k, r = KROWS, KROWS + RROWS
                rows = jnp.concatenate([rows[:k], other[:k], rows[k:r], other[k:r]], 0)
            else:
                rows = jnp.concatenate((rows,) + theirs, 0)
    with jax.named_scope("gather_core"):
        return rows, lax.ppermute(rows, "gy", [(k ^ 1, k) for k in range(NGY)])


def element_sums(nodes):
    low = nodes[:, 0] + nodes[:, 1]
    low = low[:, :-1] + low[:, 1:]
    low = low[:, :, :-1] + low[:, :, 1:]
    return low.reshape(96)


def per_device(ref_image, deformed_image, nodal_disp):
    dzlo, dzhi = from_low(deformed_image, "gz"), from_high(deformed_image, "gz")
    rzlo, rzhi = from_low(ref_image[BZ - 1:], "gz"), from_high(ref_image[:1], "gz")
    summed = element_sums(nodal_disp)
    where = jnp.stack([lax.axis_index("gz"), lax.axis_index("gy"), lax.axis_index("gx")])
    dzlo, dzhi, rzlo, rzhi, summed = lax.optimization_barrier((dzlo, dzhi, rzlo, rzhi, summed))
    planes_ = (dzlo, deformed_image, dzhi)
    up = [v[:, BY - E:, :] for v in planes_] + [ref_image[:, BY - 1, :][None]]
    down = [v[:, :E, :] for v in planes_] + [ref_image[:, 0, :][None]]
    dylo = from_low(jnp.concatenate(up, 0), "gy")
    dyhi = from_high(jnp.concatenate(down, 0), "gy")
    blocks = (deformed_image, dzlo, dzhi, dylo, dyhi)
    first, last = strips(ref_image, *blocks)
    dxlo, dxhi = from_low(last, "gx"), from_high(first, "gx")
    inside = inner(lax.optimization_barrier((summed, first))[0], *blocks)
    rows = terms(summed, ref_image, rzlo, rzhi, *blocks, dxlo, dxhi, inside)
    return tuple(solve(where, gather(rows)))


def solution(mesh):
    spec3 = P("gz", "gy", "gx")
    spec4 = P(None, "gz", "gy", "gx")
    return jax.shard_map(
        per_device, mesh=mesh, in_specs=(spec3, spec3, spec4), out_specs=(spec4, spec4),
        check_vma=False,
    )
```

```python
import jax
import jax.numpy as jnp
import numpy as np
from jax import lax
from jax.experimental import pallas as pl
from jax.experimental.pallas import tpu as pltpu
from jax.sharding import PartitionSpec as P

E = 16
CGSTEPS = 8
QUANTUM = 64
DAMPING = 0.5
BZ, BY, BX = 16, 64, 128
NGZ, NGY, NGX = 4, 8, 4
JY, JX = 5, 9
BLK = JY * JX
HI = lax.Precision.HIGHEST
PAIRS = ((0, 0), (0, 1), (0, 2), (1, 1), (1, 2), (2, 2))
PAIR_OF = {(0, 0): 0, (0, 1): 1, (0, 2): 2, (1, 1): 3, (1, 2): 4, (2, 2): 5}
KROWS = 24
RROWS = 4
F32 = jnp.float32

_T = (np.arange(E) + 0.5) / E
_W0, _W1 = 1.0 - _T, _T


def _place(kinds, count):
    low, high, mixed = kinds
    rows = np.zeros((count + 1 + (count if mixed is not None else 0), count * E), np.float32)
    for e in range(count):
        rows[e, e * E:(e + 1) * E] += low
        rows[e + 1, e * E:(e + 1) * E] += high
        if mixed is not None:
            rows[count + 1 + e, e * E:(e + 1) * E] = mixed
    return rows


def _left(rows, fields):
    out = np.zeros((rows.shape[0] * 8, fields * BY), np.float32)
    for q in range(rows.shape[0]):
        for f in range(fields):
            out[q * 8 + f, f * BY:(f + 1) * BY] = rows[q]
    return out


def _right(rows, scale):
    out = np.zeros((BX, BX), np.float32)
    out[:, :rows.shape[0]] = rows.T * scale
    return out


_SQ = (_W0 * _W0, _W1 * _W1, _W0 * _W1)
_LIN = (_W0, _W1, None)
LEFT_K = _left(_place(_SQ, 4), 6)
RIGHT_K = _right(_place(_SQ, 8), 0.25 / E**2)
LEFT_R = _left(_place(_LIN, 4), 3)
RIGHT_R = _right(_place(_LIN, 8), 0.5 / E**2)


def lanes(shape=(8, BX)):
    return lax.broadcasted_iota(jnp.int32, shape, len(shape) - 1)


def roll(x, amount, axis=1):
    size = x.shape[axis]
    if isinstance(amount, int):
        amount %= size
        if amount == 0:
            return x
    return pltpu.roll(x, amount, axis)


VMEM = pl.BlockSpec(memory_space=pltpu.VMEM)
SMEM = pl.BlockSpec(memory_space=pltpu.SMEM)


def grant(mib):
    return pltpu.CompilerParams(vmem_limit_bytes=mib << 20)


PZ, PY = 3 * E, BY + 2 * E
GROUP = PZ // 8
STRIP = GROUP * PY + BY


def piece(blocks, z, tile):
    mid, zlo, zhi, ylo, yhi = blocks
    if tile < 2:
        return ylo[z, tile * 8:tile * 8 + 8, :]
    if tile >= 10:
        return yhi[z, (tile - 10) * 8:(tile - 10) * 8 + 8, :]
    return (zlo, mid, zhi)[z // E][z % E, (tile - 2) * 8:(tile - 2) * 8 + 8, :]


def strips_kernel(ref, mid, zlo, zhi, ylo, yhi, first, last):
    blocks = (mid, zlo, zhi, ylo, yhi)
    lane = lanes()
    for zz in range(GROUP):
        for tile in range(PY // 8):
            a = jnp.zeros((8, BX), F32)
            b = jnp.zeros((8, BX), F32)
            for g in range(8):
                v = piece(blocks, g * GROUP + zz, tile)
                mask = (lane >= 16 * g) & (lane < 16 * g + 16)
                a = jnp.where(mask, roll(v, 16 * g), a)
                b = jnp.where(mask, roll(v, 16 * g + 16), b)
            row = zz * PY + tile * 8
            first[row:row + 8, :] = a
            last[row:row + 8, :] = b
    for tile in range(BY // 8):
        a = jnp.zeros((8, BX), F32)
        b = jnp.zeros((8, BX), F32)
        for z in range(BZ):
            v = ref[z, tile * 8:tile * 8 + 8, :]
            a = jnp.where(lane == z, roll(v, z), a)
            b = jnp.where(lane == z, roll(v, z + 1), b)
        row = GROUP * PY + tile * 8
        first[row:row + 8, :] = a
        last[row:row + 8, :] = b


def strips(ref, *blocks):
    shape = jax.ShapeDtypeStruct((STRIP, BX), F32)
    return pl.pallas_call(
        strips_kernel,
        out_shape=[shape, shape],
        in_specs=[VMEM] * 6,
        out_specs=[VMEM] * 2,
        compiler_params=grant(8),
        name="strips",
    )(ref, *blocks)


def warp_element(summed, tile, ey, ex, warped):
    lane = lanes((E, BX))
    e = ey * 8 + ex
    sz, sy, sx = summed[e], summed[32 + e], summed[64 + e]
    whole_z = lax.shift_right_arithmetic(sz, 9)
    whole_y = lax.shift_right_arithmetic(sy, 9)
    whole_x = lax.shift_right_arithmetic(sx, 9)
    scale = 1.0 / (8.0 * QUANTUM)
    fz = (sz & 511).astype(F32) * scale
    fy = (sy & 511).astype(F32) * scale
    fx = (sx & 511).astype(F32) * scale
    start_z = whole_z + E
    start_y = whole_y + E + ey * E
    turn = jnp.where(whole_x > 0, BX - whole_x, -whole_x)
    mask = (lane >= ex * 16) & (lane < ex * 16 + 16)
    row = pl.multiple_of(ey * E, E)

    def plane(k):
        a = tile[start_z + k, pl.ds(start_y, E), :]
        b = tile[start_z + k, pl.ds(start_y + 1, E), :]
        return (1.0 - fy) * a + fy * b

    below = plane(0)
    for k in range(E):
        above = plane(k + 1)
        v = (1.0 - fz) * below + fz * above
        v = pltpu.roll(v, turn, 1)
        v = (1.0 - fx) * v + fx * roll(v, BX - 1)
        pltpu.store(warped.at[k, pl.ds(row, E), :], v, mask=mask)
        below = above


def inner_kernel(summed, mid, zlo, zhi, ylo, yhi, warped, tile):
    blocks = (mid, zlo, zhi, ylo, yhi)
    for z in range(PZ):
        for t in range(PY // 8):
            tile[z, t * 8:t * 8 + 8, :] = piece(blocks, z, t)

    def pair(i, carry):
        for ex in range(2):
            warp_element(summed, tile, i // 3, 1 + 2 * (i % 3) + ex, warped)
        return carry

    lax.fori_loop(0, 12, pair, 0)


def inner(summed, *blocks):
    return pl.pallas_call(
        inner_kernel,
        out_shape=jax.ShapeDtypeStruct((BZ, BY, BX), F32),
        in_specs=[SMEM] + [VMEM] * 5,
        out_specs=VMEM,
        scratch_shapes=[pltpu.VMEM((PZ, PY, BX), F32)],
        compiler_params=grant(10),
        name="inner",
    )(summed, *blocks)


def slopes(pad, xlo, xhi, z, y, lane):
    here = pad[z + 1, pl.ds(8 + y, 8), :]
    along_z = pad[z + 2, pl.ds(8 + y, 8), :] - pad[z, pl.ds(8 + y, 8), :]
    along_y = pad[z + 1, pl.ds(9 + y, 8), :] - pad[z + 1, pl.ds(7 + y, 8), :]
    after_ = jnp.where(lane == BX - 1, roll(xhi, BX - 1 - z), roll(here, BX - 1))
    before = jnp.where(lane == 0, roll(xlo, -z), roll(here, 1))
    return (along_z, along_y, after_ - before), here


def terms_kernel(
    summed, ref, rzlo, rzhi, mid, zlo, zhi, ylo, yhi, xlo, xhi, inside,
    left_k, right_k, left_r, right_r, out, pad, tiles, warped, acc_k, acc_r,
):
    blocks = (mid, zlo, zhi, ylo, yhi)
    lane = lanes()
    pad[1:BZ + 1, 8:8 + BY, :] = ref[...]
    pad[0:1, 8:8 + BY, :] = rzlo[...]
    pad[BZ + 1:BZ + 2, 8:8 + BY, :] = rzhi[...]
    for z in range(BZ):
        pad[z + 1, 7:8, :] = ylo[PZ, z:z + 1, :]
        pad[z + 1, 8 + BY:9 + BY, :] = yhi[PZ, z:z + 1, :]
    for z in range(PZ):
        g, zz = z // GROUP, z % GROUP
        for t in range(PY // 8):
            v = piece(blocks, z, t)
            row = zz * PY + t * 8
            low, high = xlo[row:row + 8, :], xhi[row:row + 8, :]
            tiles[0, z, t * 8:t * 8 + 8, :] = jnp.where(lane >= 112, roll(low, 112 - 16 * g), v)
            tiles[1, z, t * 8:t * 8 + 8, :] = jnp.where(lane < 16, roll(high, -16 * g), v)

    def element(ey, carry):
        warp_element(summed, tiles.at[0], ey, 0, warped)
        warp_element(summed, tiles.at[1], ey, 7, warped)
        return carry

    lax.fori_loop(0, 4, element, 0)
    middle = (lane >= 16) & (lane < 112)

    def rows(step, carry):
        y = pl.multiple_of(step * 8, 8)
        face = pl.multiple_of(GROUP * PY + y, 8)
        low, high = xlo[pl.ds(face, 8), :], xhi[pl.ds(face, 8), :]
        sums = [[None] * 6 for _ in range(3)]
        sums_r = [[None] * 3 for _ in range(2)]

        def add(where, k, i, term):
            where[k][i] = term if where[k][i] is None else where[k][i] + term

        for z in range(BZ):
            g, here = slopes(pad, low, high, z, y, lane)
            for p, (c, d) in enumerate(PAIRS):
                product = g[c] * g[d]
                for k in range(3):
                    add(sums, k, p, product * float(_SQ[k][z]))
            moved = jnp.where(middle, inside[z, pl.ds(y, 8), :], warped[z, pl.ds(y, 8), :])
            mismatch = here - moved
            for c in range(3):
                product = g[c] * mismatch
                for k in range(2):
                    add(sums_r, k, c, product * float(_LIN[k][z]))
        for k in range(3):
            for p in range(6):
                acc_k[k, pl.ds(p * BY + y, 8), :] = sums[k][p]
        for k in range(2):
            for c in range(3):
                acc_r[k, pl.ds(c * BY + y, 8), :] = sums_r[k][c]
        return carry

    lax.fori_loop(0, BY // 8, rows, 0)

    def contract(left, fields, right):
        half = jnp.dot(left[...], fields, precision=HI, preferred_element_type=F32)
        return jnp.dot(half, right[...], precision=HI, preferred_element_type=F32)

    packed = [jnp.zeros((8, BX), F32) for _ in range(5)]
    for k in range(3):
        full = contract(left_k, acc_k[k], right_k)
        kz = 1 if k == 2 else 0
        for q in range(9):
            ky, jy = (0, q) if q < 5 else (1, q - 5)
            rows_ = full[q * 8:q * 8 + 8]
            for kx in range(2):
                if kz == 0:
                    row, base = ky * 2 + kx, BLK * k
                elif ky == 1:
                    row, base = 1 - kx, 90
                else:
                    row, base = 2 + kx, 81
                source = 0 if kx == 0 else 9
                width = 9 if kx == 0 else 8
                part = jnp.where((lane >= source) & (lane < source + width), rows_, 0.0)
                packed[row] = packed[row] + roll(part, base + jy * JX - source)
    for k in range(2):
        full = contract(left_r, acc_r[k], right_r)
        for jy in range(JY):
            part = jnp.where(lane < JX, full[jy * 8:jy * 8 + 8], 0.0)
            packed[4] = packed[4] + roll(part, BLK * k + jy * JX)
    for row in range(4):
        out[row * 6:row * 6 + 6, :] = packed[row][0:6]
    out[KROWS:KROWS + 8, :] = packed[4]


def terms(summed, *arrays):
    return pl.pallas_call(
        terms_kernel,
        out_shape=jax.ShapeDtypeStruct((KROWS + 8, BX), F32),
        in_specs=[SMEM] + [VMEM] * 15,
        out_specs=VMEM,
        scratch_shapes=[
            pltpu.VMEM((BZ + 2, BY + 16, BX), F32),
            pltpu.VMEM((2, PZ, PY, BX), F32),
            pltpu.VMEM((BZ, BY, BX), F32),
            pltpu.VMEM((3, 6 * BY, BX), F32),
            pltpu.VMEM((2, 3 * BY, BX), F32),
        ],
        compiler_params=grant(20),
        name="terms",
    )(summed, *arrays, jnp.asarray(LEFT_K), jnp.asarray(RIGHT_K),
      jnp.asarray(LEFT_R), jnp.asarray(RIGHT_R))


NZ = NGZ + 1
TILES = NZ * 2


SLOTS0 = 54 * TILES
SLOTS = SLOTS0 + 54 * 2 * NGZ


STEPS = (("gz", (1, 2, 3)), ("gx", (2,)), ("gy", (2, 4, 6)), ("gx", (1, -1)))
SIZE = {"gz": NGZ, "gx": NGX, "gy": NGY}
QUAD = NGZ * (KROWS + RROWS)


def units():
    held = [(0, 0)]
    for axis, shifts in STEPS[1:]:
        n = len(held) // 2
        groups = (held[:n], held[n:]) if shifts == (1, -1) else (held,) * len(shifts)
        for group, s in zip(groups, shifts):
            dx, dy = (s, 0) if axis == "gx" else (0, s)
            held = held + [((x + dx) % NGX, (y + dy) % NGY) for x, y in group]
    assert sorted(held) == [(x, y) for x in range(NGX) for y in range(0, NGY, 2)]
    return held


def runs():
    out = []
    for i, (dx, dy) in enumerate(units()):
        place = (dx & 1) * 2 + (dx >> 1)
        if out and out[-1][1] + out[-1][2] == place and out[-1][3] == dy:
            out[-1][2] += 1
        else:
            out.append([i, place, 1, dy])
    return out


def brick(buf, where, gz, gx, row, rhs):
    dz, dx = (gz - where[0]) & 3, (gx - where[2]) & 3
    first = NGZ * KROWS + dz * RROWS if rhs else dz * KROWS
    return buf[((dx & 1) * 2 + (dx >> 1)) * QUAD + first + row]


def stencil_slot(kz, oy, ox, pair, i):
    slot = ((oy + 1) * 3 + ox + 1) * 6 + pair
    return slot * TILES + i if kz == 0 else SLOTS0 + slot * 2 * NGZ + i


def planes(s, width):
    lane = lanes()
    zero = jnp.zeros((8, BX), F32)
    out = []
    for z in range(NZ):
        for h in range(2):
            e, o = zero, zero
            if z < NGZ:
                e = s[z][2 * h]
                o = roll(s[z][2 * h + 1], BLK)
            if z > 0:
                e = e + roll(s[z - 1][2 * h], -BLK)
                o = o + s[z - 1][2 * h + 1]
            odd = (lane >= BLK) & (lane < BLK + width)
            out.append(jnp.where(lane < width, e, jnp.where(odd, o, zero)))
    return out


def edges(s, base, width):
    lane = lanes()
    out = []
    for z in range(NGZ):
        for h in range(2):
            e = roll(s[z][2 * h], -base)
            o = roll(s[z][2 * h + 1], BLK - base)
            odd = (lane >= BLK) & (lane < BLK + width)
            out.append(jnp.where(lane < width, e, jnp.where(odd, o, 0.0)))
    return out


def cg_kernel(
    where, part0, part1, out_x, out_r, buf, stencil, shifted, xs, rs, ys, sems,
):
    own_z, own_y, own_x = where[0], where[1], where[2]
    copies = []
    for side, part in enumerate((part0, part1)):
        for first, place, count, dy in runs():
            gy = ((own_y ^ side) + dy) & 7
            copies.append(pltpu.make_async_copy(
                part.at[first * QUAD:(first + count) * QUAD, :],
                buf.at[place * QUAD:(place + count) * QUAD, gy, :],
                sems.at[len(copies)]))
    for copy in copies:
        copy.start()
    for copy in copies:
        copy.wait()

    def build(pair, carry):
        for row in range(4):
            s = [[brick(buf, where, gz, gx, row * 6 + pair, False) for gx in range(NGX)]
                 for gz in range(NGZ)]
            upper = (1, 1, 0, 0)[row]
            sides = (
                (0, row >> 1, row & 1, planes(s, 36 if row >> 1 else BLK)),
                (1, upper, (1, 0, 0, 1)[row],
                 edges(s, 90 if upper else 81, 36 if upper else BLK)),
            )
            for kz, ky, kx, field in sides:
                for oy in ((0,) if ky == 0 else (1, -1)):
                    for ox in ((0,) if kx == 0 else (1, -1)):
                        amount = (JX if oy == -1 else 0) + (1 if ox == 1 else 0)
                        for i, v in enumerate(field):
                            stencil[stencil_slot(kz, oy, ox, pair, i)] = roll(v, amount)
        return carry

    lax.fori_loop(0, 6, build, 0)
    lane = lanes()
    sub = lax.broadcasted_iota(jnp.int32, (8, BX), 0)
    even, odd = lane < BLK, (lane >= BLK) & (lane < 2 * BLK)
    zero = jnp.zeros((8, BX), F32)

    def fold(c, z, y0, y1):
        a = y0 + jnp.where(m_odd0, roll(y0, 37), 0.0) + jnp.where(m_even8, roll(y0, -37), 0.0)
        b = y1 + jnp.where(m_odd0, roll(y1, 37), 0.0) + jnp.where(m_even8, roll(y1, -37), 0.0)
        a = a + jnp.where(m_odd8, roll(y1, 53), 0.0)
        b = b + jnp.where(m_even0, roll(y0, -53), 0.0)
        out = []
        for v in (a, b):
            up = roll(roll(v, 36), 7, 0)
            down = roll(roll(v, -36), 1, 0)
            out.append(v + jnp.where(m_top, up, 0.0) + jnp.where(m_bottom, down, 0.0))
        return out

    inside = lax.rem(lane, BLK)
    jy = inside // JX
    jx = lax.rem(inside, JX)
    m_odd0, m_odd8 = odd & (jx == 0), odd & (jx == 8)
    m_even0, m_even8 = even & (jx == 0), even & (jx == 8)
    valid = lane < 2 * BLK
    m_top = valid & (jy == 4) & (sub < 7)
    m_bottom = valid & (jy == 0) & (sub > 0)
    base = valid & ((jy < 4) | (sub == 7))
    owner = (
        jnp.where(base & (jx < 8), 1.0, 0.0),
        jnp.where(base & ((jx < 8) | odd), 1.0, 0.0),
    )

    def total(v):
        return jnp.sum(jnp.sum(v, axis=1, keepdims=True), axis=0, keepdims=True)

    part = [zero, zero]
    for c in range(3):
        s = [[brick(buf, where, gz, gx, c, True) for gx in range(NGX)] for gz in range(NGZ)]
        field = planes(s, BLK)
        for z in range(NZ):
            pair_ = fold(c, z, field[2 * z], field[2 * z + 1])
            for h in range(2):
                v = pair_[h]
                i = 2 * z + h
                rs[c, i] = v
                xs[c, i] = zero
                shifted[c, 1, i] = v
                shifted[c, 0, i] = roll(v, JX)
                shifted[c, 2, i] = roll(v, -JX)
                part[h] = part[h] + v * v
    norm = total(part[0] * owner[0] + part[1] * owner[1])

    def step(_, norm_now):
        part = [zero, zero]
        for z in range(NZ):
            for h in range(2):
                sums = [[None] * 3 for _ in range(3)]
                for oz in (-1, 0, 1):
                    if not 0 <= z + oz < NZ:
                        continue
                    kz = 0 if oz == 0 else 1
                    kt = (z - 1 if oz == -1 else z) * 2 + h
                    for oy in range(3):
                        p = [shifted[d, oy, (z + oz) * 2 + h] for d in range(3)]
                        for ox in range(3):
                            k = [stencil[stencil_slot(kz, oy - 1, ox - 1, q, kt)] for q in range(6)]
                            for c in range(3):
                                for d in range(3):
                                    term = k[PAIR_OF[min(c, d), max(c, d)]] * p[d]
                                    old = sums[c][ox]
                                    sums[c][ox] = term if old is None else old + term
                for c in range(3):
                    ys[c, 2 * z + h] = sums[c][1] + roll(sums[c][0], 1) + roll(sums[c][2], -1)
            for c in range(3):
                pair_ = fold(c, z, ys[c, 2 * z], ys[c, 2 * z + 1])
                for h in range(2):
                    i = 2 * z + h
                    p = shifted[c, 1, i]
                    v = pair_[h] + DAMPING * p
                    ys[c, i] = v
                    part[h] = part[h] + v * p
        alpha = norm_now / total(part[0] * owner[0] + part[1] * owner[1])
        part = [zero, zero]
        for c in range(3):
            for i in range(TILES):
                xs[c, i] = xs[c, i] + alpha * shifted[c, 1, i]
                r = rs[c, i] - alpha * ys[c, i]
                rs[c, i] = r
                part[i % 2] = part[i % 2] + r * r
        norm_next = total(part[0] * owner[0] + part[1] * owner[1])
        beta = norm_next / norm_now
        for c in range(3):
            for i in range(TILES):
                p = rs[c, i] + beta * shifted[c, 1, i]
                shifted[c, 1, i] = p
                shifted[c, 0, i] = roll(p, JX)
                shifted[c, 2, i] = roll(p, -JX)
        return norm_next

    lax.fori_loop(0, CGSTEPS, step, norm)

    half, side = own_x >> 1, own_x & 1
    turn = jnp.where(side == 1, BX - BLK, 0)
    for src, dst, scale in ((xs, out_x, float(QUANTUM)), (rs, out_r, 1.0)):
        for c in range(3):
            for jz in range(2):
                v = src[c, (own_z + jz) * 2 + half]
                v = pltpu.roll(pltpu.roll(v, turn, 1), (8 - own_y) & 7, 0) * scale
                tile = zero
                for j in range(JY):
                    row = roll(roll(v, -j * JX), j, 0)
                    tile = jnp.where(sub == j, row, tile)
                dst[c, :, jz, :] = tile[0:JY, 0:JX]


def solve(where, parts):
    shape = jax.ShapeDtypeStruct((3, JY, 2, JX), F32)
    field = pltpu.VMEM((3, TILES, 8, BX), F32)
    return pl.pallas_call(
        cg_kernel,
        out_shape=[shape, shape],
        in_specs=[SMEM] + [VMEM] * 2,
        out_specs=[VMEM, VMEM],
        scratch_shapes=[
            pltpu.VMEM((NGX * QUAD, 8, BX), F32),
            pltpu.VMEM((SLOTS, 8, BX), F32),
            pltpu.VMEM((3, 3, TILES, 8, BX), F32),
            field, field, field,
            pltpu.SemaphoreType.DMA((2 * len(runs()),)),
        ],
        compiler_params=grant(20),
        name="cg",
    )(where, *parts)


def from_low(x, axis):
    n = lax.axis_size(axis)
    return lax.ppermute(x, axis, [(i, i + 1) for i in range(n - 1)])


def from_high(x, axis):
    n = lax.axis_size(axis)
    return lax.ppermute(x, axis, [(i + 1, i) for i in range(n - 1)])


def along_y(up, down):
    even = lax.axis_index("gy") % 2 == 0
    out = [(k, k + 1) for k in range(1, NGY - 1, 2)]
    near = [(k, k ^ 1) for k in range(NGY)]
    outer = lax.ppermute(jnp.where(even, down, up), "gy", out + [(b, a) for a, b in out])
    inner_ = lax.ppermute(jnp.where(even, up, down), "gy", near)
    return jnp.where(even, outer, inner_), jnp.where(even, inner_, outer)


def ahead(x, axis, s):
    n = lax.axis_size(axis)
    return lax.ppermute(x, axis, [((k + s) % n, k) for k in range(n)])


def gather(rows):
    for i, (axis, shifts) in enumerate(STEPS):
        with jax.named_scope("gather_" + axis + str(shifts[0])):
            n = rows.shape[0] // 2
            held = (rows[:n], rows[n:]) if shifts == (1, -1) else (rows,) * len(shifts)
            theirs = [ahead(h, axis, s) for h, s in zip(held, shifts)]
            if i == 0:
                k, r = KROWS, KROWS + RROWS
                theirs = [v[:k] for v in [rows] + theirs] + [v[k:r] for v in [rows] + theirs]
                rows = jnp.concatenate(theirs, 0)
            else:
                rows = jnp.concatenate([rows] + theirs, 0)
    with jax.named_scope("gather_core"):
        return rows, lax.ppermute(rows, "gy", [(k ^ 1, k) for k in range(NGY)])


def element_sums(nodes):
    low = nodes[:, 0] + nodes[:, 1]
    low = low[:, :-1] + low[:, 1:]
    low = low[:, :, :-1] + low[:, :, 1:]
    return low.reshape(96)


def per_device(ref_image, deformed_image, nodal_disp):
    dzlo, dzhi = from_low(deformed_image, "gz"), from_high(deformed_image, "gz")
    rzlo, rzhi = from_low(ref_image[BZ - 1:], "gz"), from_high(ref_image[:1], "gz")
    summed = element_sums(nodal_disp)
    where = jnp.stack([lax.axis_index("gz"), lax.axis_index("gy"), lax.axis_index("gx")])
    dzlo, dzhi, rzlo, rzhi, summed = lax.optimization_barrier((dzlo, dzhi, rzlo, rzhi, summed))
    planes_ = (dzlo, deformed_image, dzhi)
    up = [v[:, BY - E:, :] for v in planes_] + [ref_image[:, BY - 1, :][None]]
    down = [v[:, :E, :] for v in planes_] + [ref_image[:, 0, :][None]]
    dylo, dyhi = along_y(jnp.concatenate(up, 0), jnp.concatenate(down, 0))
    blocks = (deformed_image, dzlo, dzhi, dylo, dyhi)
    first, last = strips(ref_image, *blocks)
    dxlo, dxhi = from_low(last, "gx"), from_high(first, "gx")
    inside = inner(lax.optimization_barrier((summed, first))[0], *blocks)
    rows = terms(summed, ref_image, rzlo, rzhi, *blocks, dxlo, dxhi, inside)
    return tuple(jnp.swapaxes(v, 1, 2) for v in solve(where, gather(rows)))


def solution(mesh):
    spec3 = P("gz", "gy", "gx")
    spec4 = P(None, "gz", "gy", "gx")
    return jax.shard_map(
        per_device, mesh=mesh, in_specs=(spec3, spec3, spec4), out_specs=(spec4, spec4),
        check_vma=False,
    )
```

```python
import jax
import jax.numpy as jnp
import numpy as np
from jax import lax
from jax.experimental import pallas as pl
from jax.experimental.pallas import tpu as pltpu
from jax.sharding import PartitionSpec as P

E = 16
CGSTEPS = 8
QUANTUM = 64
DAMPING = 0.5
BZ, BY, BX = 16, 64, 128
NGZ, NGY, NGX = 4, 8, 4
JY, JX = 5, 9
BLK = JY * JX
HI = lax.Precision.HIGHEST
PAIRS = ((0, 0), (0, 1), (0, 2), (1, 1), (1, 2), (2, 2))
PAIR_OF = {(0, 0): 0, (0, 1): 1, (0, 2): 2, (1, 1): 3, (1, 2): 4, (2, 2): 5}
KROWS = 24
RROWS = 4
F32 = jnp.float32

_T = (np.arange(E) + 0.5) / E
_W0, _W1 = 1.0 - _T, _T


def _place(kinds, count):
    low, high, mixed = kinds
    rows = np.zeros((count + 1 + (count if mixed is not None else 0), count * E), np.float32)
    for e in range(count):
        rows[e, e * E:(e + 1) * E] += low
        rows[e + 1, e * E:(e + 1) * E] += high
        if mixed is not None:
            rows[count + 1 + e, e * E:(e + 1) * E] = mixed
    return rows


def _left(rows, fields):
    out = np.zeros((rows.shape[0] * 8, fields * BY), np.float32)
    for q in range(rows.shape[0]):
        for f in range(fields):
            out[q * 8 + f, f * BY:(f + 1) * BY] = rows[q]
    return out


def _right(rows, scale):
    out = np.zeros((BX, BX), np.float32)
    out[:, :rows.shape[0]] = rows.T * scale
    return out


_SQ = (_W0 * _W0, _W1 * _W1, _W0 * _W1)
_LIN = (_W0, _W1, None)
LEFT_K = _left(_place(_SQ, 4), 6)
RIGHT_K = _right(_place(_SQ, 8), 0.25 / E**2)
LEFT_R = _left(_place(_LIN, 4), 3)
RIGHT_R = _right(_place(_LIN, 8), 0.5 / E**2)


def lanes(shape=(8, BX)):
    return lax.broadcasted_iota(jnp.int32, shape, len(shape) - 1)


def roll(x, amount, axis=1):
    size = x.shape[axis]
    if isinstance(amount, int):
        amount %= size
        if amount == 0:
            return x
    return pltpu.roll(x, amount, axis)


VMEM = pl.BlockSpec(memory_space=pltpu.VMEM)
SMEM = pl.BlockSpec(memory_space=pltpu.SMEM)


def grant(mib):
    return pltpu.CompilerParams(vmem_limit_bytes=mib << 20)


PZ, PY = 3 * E, BY + 2 * E
GROUP = PZ // 8
STRIP = GROUP * PY + 8


def piece(blocks, z, tile):
    mid, zlo, zhi, ylo, yhi = blocks
    if tile < 2:
        return ylo[z, tile * 8:tile * 8 + 8, :]
    if tile >= 10:
        return yhi[z, (tile - 10) * 8:(tile - 10) * 8 + 8, :]
    return (zlo, mid, zhi)[z // E][z % E, (tile - 2) * 8:(tile - 2) * 8 + 8, :]


def columns(lane, g):
    return (lane >= 16 * g) & (lane < 16 * g + 16)


def strips_kernel(ref, mid, zlo, zhi, ylo, yhi, first, last):
    blocks = (mid, zlo, zhi, ylo, yhi)
    lane = lanes()
    for zz in range(GROUP):
        for tile in range(PY // 8):
            a = jnp.zeros((8, BX), F32)
            b = jnp.zeros((8, BX), F32)
            for g in range(8):
                v = piece(blocks, g * GROUP + zz, tile)
                v = roll(v, 16 * g)
                a = jnp.where(columns(lane, g), v, a)
                b = jnp.where(columns(lane, (g + 7) % 8), v, b)
            row = zz * PY + tile * 8
            first[row:row + 8, :] = a
            last[row:row + 8, :] = b
    a = jnp.zeros((8, BX), F32)
    b = jnp.zeros((8, BX), F32)
    for tile in range(BY // 8):
        for z in range(BZ):
            v = ref[z, tile * 8:tile * 8 + 8, :]
            to = 16 * tile + z
            a = jnp.where(lane == to, roll(v, to), a)
            b = jnp.where(lane == to, roll(v, to + 1), b)
    first[GROUP * PY:, :] = a
    last[GROUP * PY:, :] = b


def strips(ref, *blocks):
    shape = jax.ShapeDtypeStruct((STRIP, BX), F32)
    return pl.pallas_call(
        strips_kernel,
        out_shape=[shape, shape],
        in_specs=[VMEM] * 6,
        out_specs=[VMEM] * 2,
        compiler_params=grant(8),
        name="strips",
    )(ref, *blocks)


def warp_element(summed, tile, ey, ex, warped):
    lane = lanes((E, BX))
    e = ey * 8 + ex
    sz, sy, sx = summed[e], summed[32 + e], summed[64 + e]
    whole_z = lax.shift_right_arithmetic(sz, 9)
    whole_y = lax.shift_right_arithmetic(sy, 9)
    whole_x = lax.shift_right_arithmetic(sx, 9)
    scale = 1.0 / (8.0 * QUANTUM)
    fz = (sz & 511).astype(F32) * scale
    fy = (sy & 511).astype(F32) * scale
    fx = (sx & 511).astype(F32) * scale
    start_z = whole_z + E
    start_y = whole_y + E + ey * E
    turn = jnp.where(whole_x > 0, BX - whole_x, -whole_x)
    mask = (lane >= ex * 16) & (lane < ex * 16 + 16)
    row = pl.multiple_of(ey * E, E)

    def plane(k):
        a = tile[start_z + k, pl.ds(start_y, E), :]
        b = tile[start_z + k, pl.ds(start_y + 1, E), :]
        return (1.0 - fy) * a + fy * b

    below = plane(0)
    for k in range(E):
        above = plane(k + 1)
        v = (1.0 - fz) * below + fz * above
        v = pltpu.roll(v, turn, 1)
        v = (1.0 - fx) * v + fx * roll(v, BX - 1)
        pltpu.store(warped.at[k, pl.ds(row, E), :], v, mask=mask)
        below = above


def inner_kernel(summed, mid, zlo, zhi, ylo, yhi, warped, tile):
    blocks = (mid, zlo, zhi, ylo, yhi)
    for z in range(PZ):
        for t in range(PY // 8):
            tile[z, t * 8:t * 8 + 8, :] = piece(blocks, z, t)

    def pair(i, carry):
        for ex in range(2):
            warp_element(summed, tile, i // 3, 1 + 2 * (i % 3) + ex, warped)
        return carry

    lax.fori_loop(0, 12, pair, 0)


def inner(summed, *blocks):
    return pl.pallas_call(
        inner_kernel,
        out_shape=jax.ShapeDtypeStruct((BZ, BY, BX), F32),
        in_specs=[SMEM] + [VMEM] * 5,
        out_specs=VMEM,
        scratch_shapes=[pltpu.VMEM((PZ, PY, BX), F32)],
        compiler_params=grant(10),
        name="inner",
    )(summed, *blocks)


def slopes(pad, xlo, xhi, z, y, lane):
    here = pad[z + 1, pl.ds(8 + y, 8), :]
    along_z = pad[z + 2, pl.ds(8 + y, 8), :] - pad[z, pl.ds(8 + y, 8), :]
    along_y = pad[z + 1, pl.ds(9 + y, 8), :] - pad[z + 1, pl.ds(7 + y, 8), :]
    after_ = jnp.where(lane == BX - 1, roll(xhi, BX - 1 - z), roll(here, BX - 1))
    before = jnp.where(lane == 0, roll(xlo, -z), roll(here, 1))
    return (along_z, along_y, after_ - before), here


def terms_kernel(
    summed, ref, rzlo, rzhi, mid, zlo, zhi, ylo, yhi, xlo, xhi, inside,
    left_k, right_k, left_r, right_r, out, pad, tiles, warped, acc_k, acc_r,
):
    blocks = (mid, zlo, zhi, ylo, yhi)
    lane = lanes()
    pad[1:BZ + 1, 8:8 + BY, :] = ref[...]
    pad[0:1, 8:8 + BY, :] = rzlo[...]
    pad[BZ + 1:BZ + 2, 8:8 + BY, :] = rzhi[...]
    for z in range(BZ):
        pad[z + 1, 7:8, :] = ylo[PZ, z:z + 1, :]
        pad[z + 1, 8 + BY:9 + BY, :] = yhi[PZ, z:z + 1, :]
    for z in range(PZ):
        g, zz = z // GROUP, z % GROUP
        for t in range(PY // 8):
            v = piece(blocks, z, t)
            row = zz * PY + t * 8
            both = jnp.where(columns(lane, (g + 7) % 8), xlo[row:row + 8, :], xhi[row:row + 8, :])
            both = roll(both, -16 * g)
            tiles[0, z, t * 8:t * 8 + 8, :] = jnp.where(lane >= 112, both, v)
            tiles[1, z, t * 8:t * 8 + 8, :] = jnp.where(lane < 16, both, v)

    def element(ey, carry):
        warp_element(summed, tiles.at[0], ey, 0, warped)
        warp_element(summed, tiles.at[1], ey, 7, warped)
        return carry

    lax.fori_loop(0, 4, element, 0)
    middle = (lane >= 16) & (lane < 112)

    def rows(step, carry):
        y = pl.multiple_of(step * 8, 8)
        low = pltpu.roll(xlo[GROUP * PY:, :], (8 - step) % 8 * 16, 1)
        high = pltpu.roll(xhi[GROUP * PY:, :], (8 - step) % 8 * 16, 1)
        sums = [[None] * 6 for _ in range(3)]
        sums_r = [[None] * 3 for _ in range(2)]

        def add(where, k, i, term):
            where[k][i] = term if where[k][i] is None else where[k][i] + term

        for z in range(BZ):
            g, here = slopes(pad, low, high, z, y, lane)
            for p, (c, d) in enumerate(PAIRS):
                product = g[c] * g[d]
                for k in range(3):
                    add(sums, k, p, product * float(_SQ[k][z]))
            moved = jnp.where(middle, inside[z, pl.ds(y, 8), :], warped[z, pl.ds(y, 8), :])
            mismatch = here - moved
            for c in range(3):
                product = g[c] * mismatch
                for k in range(2):
                    add(sums_r, k, c, product * float(_LIN[k][z]))
        for k in range(3):
            for p in range(6):
                acc_k[k, pl.ds(p * BY + y, 8), :] = sums[k][p]
        for k in range(2):
            for c in range(3):
                acc_r[k, pl.ds(c * BY + y, 8), :] = sums_r[k][c]
        return carry

    lax.fori_loop(0, BY // 8, rows, 0)

    def contract(left, fields, right):
        half = jnp.dot(left[...], fields, precision=HI, preferred_element_type=F32)
        return jnp.dot(half, right[...], precision=HI, preferred_element_type=F32)

    packed = [jnp.zeros((8, BX), F32) for _ in range(5)]
    for k in range(3):
        full = contract(left_k, acc_k[k], right_k)
        kz = 1 if k == 2 else 0
        for q in range(9):
            ky, jy = (0, q) if q < 5 else (1, q - 5)
            rows_ = full[q * 8:q * 8 + 8]
            for kx in range(2):
                if kz == 0:
                    row, base = ky * 2 + kx, BLK * k
                elif ky == 1:
                    row, base = 1 - kx, 90
                else:
                    row, base = 2 + kx, 81
                source = 0 if kx == 0 else 9
                width = 9 if kx == 0 else 8
                part = jnp.where((lane >= source) & (lane < source + width), rows_, 0.0)
                packed[row] = packed[row] + roll(part, base + jy * JX - source)
    for k in range(2):
        full = contract(left_r, acc_r[k], right_r)
        for jy in range(JY):
            part = jnp.where(lane < JX, full[jy * 8:jy * 8 + 8], 0.0)
            packed[4] = packed[4] + roll(part, BLK * k + jy * JX)
    for row in range(4):
        out[row * 6:row * 6 + 6, :] = packed[row][0:6]
    out[KROWS:KROWS + 8, :] = packed[4]


def terms(summed, *arrays):
    return pl.pallas_call(
        terms_kernel,
        out_shape=jax.ShapeDtypeStruct((KROWS + 8, BX), F32),
        in_specs=[SMEM] + [VMEM] * 15,
        out_specs=VMEM,
        scratch_shapes=[
            pltpu.VMEM((BZ + 2, BY + 16, BX), F32),
            pltpu.VMEM((2, PZ, PY, BX), F32),
            pltpu.VMEM((BZ, BY, BX), F32),
            pltpu.VMEM((3, 6 * BY, BX), F32),
            pltpu.VMEM((2, 3 * BY, BX), F32),
        ],
        compiler_params=grant(20),
        name="terms",
    )(summed, *arrays, jnp.asarray(LEFT_K), jnp.asarray(RIGHT_K),
      jnp.asarray(LEFT_R), jnp.asarray(RIGHT_R))


NZ = NGZ + 1
TILES = NZ * 2


SLOTS0 = 54 * TILES
SLOTS = SLOTS0 + 54 * 2 * NGZ


STEPS = (("gz", (1, 2, 3)), ("gx", (2,)), ("gy", (2, 4, 6)), ("gx", (1, -1)))
SIZE = {"gz": NGZ, "gx": NGX, "gy": NGY}
QUAD = NGZ * (KROWS + RROWS)


def units():
    held = [(0, 0)]
    for axis, shifts in STEPS[1:]:
        n = len(held) // 2
        groups = (held[:n], held[n:]) if shifts == (1, -1) else (held,) * len(shifts)
        for group, s in zip(groups, shifts):
            dx, dy = (s, 0) if axis == "gx" else (0, s)
            held = held + [((x + dx) % NGX, (y + dy) % NGY) for x, y in group]
    assert sorted(held) == [(x, y) for x in range(NGX) for y in range(0, NGY, 2)]
    return held


def brick(buf, where, gz, gx, row, rhs):
    dz, dx = (gz - where[0]) & 3, (gx - where[2]) & 3
    first = NGZ * KROWS + dz * RROWS if rhs else dz * KROWS
    start = pl.multiple_of((((dx & 1) * 2 + (dx >> 1)) * QUAD + first + row) * 8, 8)
    return buf[pl.ds(start, 8), :]


def stencil_slot(kz, oy, ox, pair, i):
    slot = ((oy + 1) * 3 + ox + 1) * 6 + pair
    return slot * TILES + i if kz == 0 else SLOTS0 + slot * 2 * NGZ + i


def planes(s, width):
    lane = lanes()
    zero = jnp.zeros((8, BX), F32)
    out = []
    for z in range(NZ):
        for h in range(2):
            e, o = zero, zero
            if z < NGZ:
                e = s[z][2 * h]
                o = roll(s[z][2 * h + 1], BLK)
            if z > 0:
                e = e + roll(s[z - 1][2 * h], -BLK)
                o = o + s[z - 1][2 * h + 1]
            odd = (lane >= BLK) & (lane < BLK + width)
            out.append(jnp.where(lane < width, e, jnp.where(odd, o, zero)))
    return out


def edges(s, base, width):
    lane = lanes()
    out = []
    for z in range(NGZ):
        for h in range(2):
            e = roll(s[z][2 * h], -base)
            o = roll(s[z][2 * h + 1], BLK - base)
            odd = (lane >= BLK) & (lane < BLK + width)
            out.append(jnp.where(lane < width, e, jnp.where(odd, o, 0.0)))
    return out


def cg_kernel(
    where, part0, part1, out_x, out_r, buf, stencil, shifted, xs, rs, ys,
):
    own_z, own_y, own_x = where[0], where[1], where[2]
    for side, part in enumerate((part0, part1)):
        for i, (dx, dy) in enumerate(units()):
            gy = ((own_y ^ side) + dy) & 7
            place = (dx & 1) * 2 + (dx >> 1)
            for r in range(0, QUAD, 8):
                buf[pl.ds((place * QUAD + r) * 8 + gy, 8, stride=8), :] = (
                    part[i * QUAD + r:i * QUAD + r + 8, :])

    def build(pair, carry):
        for row in range(4):
            s = [[brick(buf, where, gz, gx, row * 6 + pair, False) for gx in range(NGX)]
                 for gz in range(NGZ)]
            upper = (1, 1, 0, 0)[row]
            sides = (
                (0, row >> 1, row & 1, planes(s, 36 if row >> 1 else BLK)),
                (1, upper, (1, 0, 0, 1)[row],
                 edges(s, 90 if upper else 81, 36 if upper else BLK)),
            )
            for kz, ky, kx, field in sides:
                for oy in ((0,) if ky == 0 else (1, -1)):
                    for ox in ((0,) if kx == 0 else (1, -1)):
                        amount = (JX if oy == -1 else 0) + (1 if ox == 1 else 0)
                        for i, v in enumerate(field):
                            stencil[stencil_slot(kz, oy, ox, pair, i)] = roll(v, amount)
        return carry

    lax.fori_loop(0, 6, build, 0)
    lane = lanes()
    sub = lax.broadcasted_iota(jnp.int32, (8, BX), 0)
    even, odd = lane < BLK, (lane >= BLK) & (lane < 2 * BLK)
    zero = jnp.zeros((8, BX), F32)

    def fold(c, z, y0, y1):
        a = y0 + jnp.where(m_odd0, roll(y0, 37), 0.0) + jnp.where(m_even8, roll(y0, -37), 0.0)
        b = y1 + jnp.where(m_odd0, roll(y1, 37), 0.0) + jnp.where(m_even8, roll(y1, -37), 0.0)
        a = a + jnp.where(m_odd8, roll(y1, 53), 0.0)
        b = b + jnp.where(m_even0, roll(y0, -53), 0.0)
        out = []
        for v in (a, b):
            up = roll(roll(v, 36), 7, 0)
            down = roll(roll(v, -36), 1, 0)
            out.append(v + jnp.where(m_top, up, 0.0) + jnp.where(m_bottom, down, 0.0))
        return out

    inside = lax.rem(lane, BLK)
    jy = inside // JX
    jx = lax.rem(inside, JX)
    m_odd0, m_odd8 = odd & (jx == 0), odd & (jx == 8)
    m_even0, m_even8 = even & (jx == 0), even & (jx == 8)
    valid = lane < 2 * BLK
    m_top = valid & (jy == 4) & (sub < 7)
    m_bottom = valid & (jy == 0) & (sub > 0)
    base = valid & ((jy < 4) | (sub == 7))
    owner = (
        jnp.where(base & (jx < 8), 1.0, 0.0),
        jnp.where(base & ((jx < 8) | odd), 1.0, 0.0),
    )

    def total(v):
        return jnp.sum(jnp.sum(v, axis=1, keepdims=True), axis=0, keepdims=True)

    part = [zero, zero]
    for c in range(3):
        s = [[brick(buf, where, gz, gx, c, True) for gx in range(NGX)] for gz in range(NGZ)]
        field = planes(s, BLK)
        for z in range(NZ):
            pair_ = fold(c, z, field[2 * z], field[2 * z + 1])
            for h in range(2):
                v = pair_[h]
                i = 2 * z + h
                rs[c, i] = v
                xs[c, i] = zero
                shifted[c, 1, i] = v
                shifted[c, 0, i] = roll(v, JX)
                shifted[c, 2, i] = roll(v, -JX)
                part[h] = part[h] + v * v
    norm = total(part[0] * owner[0] + part[1] * owner[1])

    def step(_, norm_now):
        part = [zero, zero]
        for z in range(NZ):
            for h in range(2):
                sums = [[None] * 3 for _ in range(3)]
                for oz in (-1, 0, 1):
                    if not 0 <= z + oz < NZ:
                        continue
                    kz = 0 if oz == 0 else 1
                    kt = (z - 1 if oz == -1 else z) * 2 + h
                    for oy in range(3):
                        p = [shifted[d, oy, (z + oz) * 2 + h] for d in range(3)]
                        for ox in range(3):
                            k = [stencil[stencil_slot(kz, oy - 1, ox - 1, q, kt)] for q in range(6)]
                            for c in range(3):
                                for d in range(3):
                                    term = k[PAIR_OF[min(c, d), max(c, d)]] * p[d]
                                    old = sums[c][ox]
                                    sums[c][ox] = term if old is None else old + term
                for c in range(3):
                    ys[c, 2 * z + h] = sums[c][1] + roll(sums[c][0], 1) + roll(sums[c][2], -1)
            for c in range(3):
                pair_ = fold(c, z, ys[c, 2 * z], ys[c, 2 * z + 1])
                for h in range(2):
                    i = 2 * z + h
                    p = shifted[c, 1, i]
                    v = pair_[h] + DAMPING * p
                    ys[c, i] = v
                    part[h] = part[h] + v * p
        alpha = norm_now / total(part[0] * owner[0] + part[1] * owner[1])
        part = [zero, zero]
        for c in range(3):
            for i in range(TILES):
                xs[c, i] = xs[c, i] + alpha * shifted[c, 1, i]
                r = rs[c, i] - alpha * ys[c, i]
                rs[c, i] = r
                part[i % 2] = part[i % 2] + r * r
        norm_next = total(part[0] * owner[0] + part[1] * owner[1])
        beta = norm_next / norm_now
        for c in range(3):
            for i in range(TILES):
                p = rs[c, i] + beta * shifted[c, 1, i]
                shifted[c, 1, i] = p
                shifted[c, 0, i] = roll(p, JX)
                shifted[c, 2, i] = roll(p, -JX)
        return norm_next

    lax.fori_loop(0, CGSTEPS, step, norm)

    half, side = own_x >> 1, own_x & 1
    turn = jnp.where(side == 1, BX - BLK, 0)
    for src, dst, scale in ((xs, out_x, float(QUANTUM)), (rs, out_r, 1.0)):
        for c in range(3):
            for jz in range(2):
                v = src[c, (own_z + jz) * 2 + half]
                v = pltpu.roll(pltpu.roll(v, turn, 1), (8 - own_y) & 7, 0) * scale
                tile = zero
                for j in range(JY):
                    row = roll(roll(v, -j * JX), j, 0)
                    tile = jnp.where(sub == j, row, tile)
                dst[c, :, jz, :] = tile[0:JY, 0:JX]


def solve(where, parts):
    shape = jax.ShapeDtypeStruct((3, JY, 2, JX), F32)
    field = pltpu.VMEM((3, TILES, 8, BX), F32)
    return pl.pallas_call(
        cg_kernel,
        out_shape=[shape, shape],
        in_specs=[SMEM] + [VMEM] * 2,
        out_specs=[VMEM, VMEM],
        scratch_shapes=[
            pltpu.VMEM((NGX * QUAD * 8, BX), F32),
            pltpu.VMEM((SLOTS, 8, BX), F32),
            pltpu.VMEM((3, 3, TILES, 8, BX), F32),
            field, field, field,
        ],
        compiler_params=grant(20),
        name="cg",
    )(where, *parts)


def from_low(x, axis):
    n = lax.axis_size(axis)
    return lax.ppermute(x, axis, [(i, i + 1) for i in range(n - 1)])


def from_high(x, axis):
    n = lax.axis_size(axis)
    return lax.ppermute(x, axis, [(i + 1, i) for i in range(n - 1)])


def along_y(up, down):
    even = lax.axis_index("gy") % 2 == 0
    out = [(k, k + 1) for k in range(1, NGY - 1, 2)]
    near = [(k, k ^ 1) for k in range(NGY)]
    outer = jnp.where(even, down, up)
    up, down, _ = lax.optimization_barrier((up, down, outer))
    inner_ = lax.ppermute(jnp.where(even, up, down), "gy", near)
    outer = lax.ppermute(outer, "gy", out + [(b, a) for a, b in out])
    return jnp.where(even, outer, inner_), jnp.where(even, inner_, outer)


def ahead(x, axis, s):
    n = lax.axis_size(axis)
    return lax.ppermute(x, axis, [((k + s) % n, k) for k in range(n)])


def gather(rows):
    for i, (axis, shifts) in enumerate(STEPS):
        with jax.named_scope("gather_" + axis + str(shifts[0])):
            n = rows.shape[0] // 2
            held = (rows[:n], rows[n:]) if shifts == (1, -1) else (rows,) * len(shifts)
            theirs = [ahead(h, axis, s) for h, s in zip(held, shifts)]
            if i == 0:
                k, r = KROWS, KROWS + RROWS
                theirs = [v[:k] for v in [rows] + theirs] + [v[k:r] for v in [rows] + theirs]
                rows = jnp.concatenate(theirs, 0)
            else:
                rows = jnp.concatenate([rows] + theirs, 0)
    with jax.named_scope("gather_core"):
        return rows, lax.ppermute(rows, "gy", [(k ^ 1, k) for k in range(NGY)])


def element_sums(nodes):
    low = nodes[:, 0] + nodes[:, 1]
    low = low[:, :-1] + low[:, 1:]
    low = low[:, :, :-1] + low[:, :, 1:]
    return low.reshape(96)


def per_device(ref_image, deformed_image, nodal_disp):
    dzlo, dzhi = from_low(deformed_image, "gz"), from_high(deformed_image, "gz")
    rzlo, rzhi = from_low(ref_image[BZ - 1:], "gz"), from_high(ref_image[:1], "gz")
    summed = element_sums(nodal_disp)
    where = jnp.stack([lax.axis_index("gz"), lax.axis_index("gy"), lax.axis_index("gx")])
    dzlo, dzhi, rzlo, rzhi, summed = lax.optimization_barrier((dzlo, dzhi, rzlo, rzhi, summed))
    planes_ = (dzlo, deformed_image, dzhi)
    up = [v[:, BY - E:, :] for v in planes_] + [ref_image[:, BY - 1, :][None]]
    down = [v[:, :E, :] for v in planes_] + [ref_image[:, 0, :][None]]
    dylo, dyhi = along_y(jnp.concatenate(up, 0), jnp.concatenate(down, 0))
    blocks = (deformed_image, dzlo, dzhi, dylo, dyhi)
    first, last = strips(ref_image, *blocks)
    dxlo, dxhi = from_low(last, "gx"), from_high(first, "gx")
    inside = inner(lax.optimization_barrier((summed, first))[0], *blocks)
    rows = terms(summed, ref_image, rzlo, rzhi, *blocks, dxlo, dxhi, inside)
    return tuple(jnp.swapaxes(v, 1, 2) for v in solve(where, gather(rows)))


def solution(mesh):
    spec3 = P("gz", "gy", "gx")
    spec4 = P(None, "gz", "gy", "gx")
    return jax.shard_map(
        per_device, mesh=mesh, in_specs=(spec3, spec3, spec4), out_specs=(spec4, spec4),
        check_vma=False,
    )
```

```python
import jax
import jax.numpy as jnp
import numpy as np
from jax import lax
from jax.experimental import pallas as pl
from jax.experimental.pallas import tpu as pltpu
from jax.sharding import PartitionSpec as P

E = 16
CGSTEPS = 8
QUANTUM = 64
DAMPING = 0.5
BZ, BY, BX = 16, 64, 128
NGZ, NGY, NGX = 4, 8, 4
JY, JX = 5, 9
BLK = JY * JX
HI = lax.Precision.HIGHEST
PAIRS = ((0, 0), (0, 1), (0, 2), (1, 1), (1, 2), (2, 2))
PAIR_OF = {(0, 0): 0, (0, 1): 1, (0, 2): 2, (1, 1): 3, (1, 2): 4, (2, 2): 5}
KROWS = 24
RROWS = 4
F32 = jnp.float32

_T = (np.arange(E) + 0.5) / E
_W0, _W1 = 1.0 - _T, _T


def _place(kinds, count):
    low, high, mixed = kinds
    rows = np.zeros((count + 1 + (count if mixed is not None else 0), count * E), np.float32)
    for e in range(count):
        rows[e, e * E:(e + 1) * E] += low
        rows[e + 1, e * E:(e + 1) * E] += high
        if mixed is not None:
            rows[count + 1 + e, e * E:(e + 1) * E] = mixed
    return rows


def _left(rows, fields):
    out = np.zeros((rows.shape[0] * 8, fields * BY), np.float32)
    for q in range(rows.shape[0]):
        for f in range(fields):
            out[q * 8 + f, f * BY:(f + 1) * BY] = rows[q]
    return out


def _right(rows, scale):
    out = np.zeros((BX, BX), np.float32)
    out[:, :rows.shape[0]] = rows.T * scale
    return out


_SQ = (_W0 * _W0, _W1 * _W1, _W0 * _W1)
_LIN = (_W0, _W1, None)
LEFT_K = _left(_place(_SQ, 4), 6)
RIGHT_K = _right(_place(_SQ, 8), 0.25 / E**2)
LEFT_R = _left(_place(_LIN, 4), 3)
RIGHT_R = _right(_place(_LIN, 8), 0.5 / E**2)


def lanes(shape=(8, BX)):
    return lax.broadcasted_iota(jnp.int32, shape, len(shape) - 1)


def roll(x, amount, axis=1):
    size = x.shape[axis]
    if isinstance(amount, int):
        amount %= size
        if amount == 0:
            return x
    return pltpu.roll(x, amount, axis)


VMEM = pl.BlockSpec(memory_space=pltpu.VMEM)
SMEM = pl.BlockSpec(memory_space=pltpu.SMEM)


def grant(mib):
    return pltpu.CompilerParams(vmem_limit_bytes=mib << 20)


PZ, PY = 3 * E, BY + 2 * E
GROUP = PZ // 8
STRIP = GROUP * PY + 8


def piece(blocks, z, tile):
    mid, zlo, zhi, ylo, yhi = blocks
    if tile < 2:
        return ylo[z, tile * 8:tile * 8 + 8, :]
    if tile >= 10:
        return yhi[z, (tile - 10) * 8:(tile - 10) * 8 + 8, :]
    return (zlo, mid, zhi)[z // E][z % E, (tile - 2) * 8:(tile - 2) * 8 + 8, :]


def columns(lane, g):
    return (lane >= 16 * g) & (lane < 16 * g + 16)


def strips_kernel(ref, mid, zlo, zhi, ylo, yhi, first, last):
    blocks = (mid, zlo, zhi, ylo, yhi)
    lane = lanes()
    for zz in range(GROUP):
        for tile in range(PY // 8):
            a = jnp.zeros((8, BX), F32)
            b = jnp.zeros((8, BX), F32)
            for g in range(8):
                v = piece(blocks, g * GROUP + zz, tile)
                v = roll(v, 16 * g)
                a = jnp.where(columns(lane, g), v, a)
                b = jnp.where(columns(lane, (g + 7) % 8), v, b)
            row = zz * PY + tile * 8
            first[row:row + 8, :] = a
            last[row:row + 8, :] = b
    a = jnp.zeros((8, BX), F32)
    b = jnp.zeros((8, BX), F32)
    for tile in range(BY // 8):
        for z in range(BZ):
            v = ref[z, tile * 8:tile * 8 + 8, :]
            to = 16 * tile + z
            a = jnp.where(lane == to, roll(v, to), a)
            b = jnp.where(lane == to, roll(v, to + 1), b)
    first[GROUP * PY:, :] = a
    last[GROUP * PY:, :] = b


def strips(ref, *blocks):
    shape = jax.ShapeDtypeStruct((STRIP, BX), F32)
    return pl.pallas_call(
        strips_kernel,
        out_shape=[shape, shape],
        in_specs=[VMEM] * 6,
        out_specs=[VMEM] * 2,
        compiler_params=grant(8),
        name="strips",
    )(ref, *blocks)


def warp_element(summed, tile, ey, ex, warped):
    lane = lanes((E, BX))
    e = ey * 8 + ex
    sz, sy, sx = summed[e], summed[32 + e], summed[64 + e]
    whole_z = lax.shift_right_arithmetic(sz, 9)
    whole_y = lax.shift_right_arithmetic(sy, 9)
    whole_x = lax.shift_right_arithmetic(sx, 9)
    scale = 1.0 / (8.0 * QUANTUM)
    fz = (sz & 511).astype(F32) * scale
    fy = (sy & 511).astype(F32) * scale
    fx = (sx & 511).astype(F32) * scale
    start_z = whole_z + E
    start_y = whole_y + E + ey * E
    turn = jnp.where(whole_x > 0, BX - whole_x, -whole_x)
    mask = (lane >= ex * 16) & (lane < ex * 16 + 16)
    row = pl.multiple_of(ey * E, E)

    def plane(k):
        a = tile[start_z + k, pl.ds(start_y, E), :]
        b = tile[start_z + k, pl.ds(start_y + 1, E), :]
        return (1.0 - fy) * a + fy * b

    below = plane(0)
    for k in range(E):
        above = plane(k + 1)
        v = (1.0 - fz) * below + fz * above
        v = pltpu.roll(v, turn, 1)
        v = (1.0 - fx) * v + fx * roll(v, BX - 1)
        pltpu.store(warped.at[k, pl.ds(row, E), :], v, mask=mask)
        below = above


def inner_kernel(summed, mid, zlo, zhi, ylo, yhi, warped, tile):
    blocks = (mid, zlo, zhi, ylo, yhi)
    for z in range(PZ):
        for t in range(PY // 8):
            tile[z, t * 8:t * 8 + 8, :] = piece(blocks, z, t)

    def pair(i, carry):
        for ex in range(2):
            warp_element(summed, tile, i // 3, 1 + 2 * (i % 3) + ex, warped)
        return carry

    lax.fori_loop(0, 12, pair, 0)


def inner(summed, *blocks):
    return pl.pallas_call(
        inner_kernel,
        out_shape=jax.ShapeDtypeStruct((BZ, BY, BX), F32),
        in_specs=[SMEM] + [VMEM] * 5,
        out_specs=VMEM,
        scratch_shapes=[pltpu.VMEM((PZ, PY, BX), F32)],
        compiler_params=grant(10),
        name="inner",
    )(summed, *blocks)


def slopes(pad, xlo, xhi, z, y, lane):
    here = pad[z + 1, pl.ds(8 + y, 8), :]
    along_z = pad[z + 2, pl.ds(8 + y, 8), :] - pad[z, pl.ds(8 + y, 8), :]
    along_y = pad[z + 1, pl.ds(9 + y, 8), :] - pad[z + 1, pl.ds(7 + y, 8), :]
    after_ = jnp.where(lane == BX - 1, roll(xhi, BX - 1 - z), roll(here, BX - 1))
    before = jnp.where(lane == 0, roll(xlo, -z), roll(here, 1))
    return (along_z, along_y, after_ - before), here


def terms_kernel(
    summed, ref, rzlo, rzhi, mid, zlo, zhi, ylo, yhi, xlo, xhi, inside,
    left_k, right_k, left_r, right_r, out, pad, tiles, warped, acc_k, acc_r,
):
    blocks = (mid, zlo, zhi, ylo, yhi)
    lane = lanes()
    pad[1:BZ + 1, 8:8 + BY, :] = ref[...]
    pad[0:1, 8:8 + BY, :] = rzlo[...]
    pad[BZ + 1:BZ + 2, 8:8 + BY, :] = rzhi[...]
    for z in range(BZ):
        pad[z + 1, 7:8, :] = ylo[PZ, z:z + 1, :]
        pad[z + 1, 8 + BY:9 + BY, :] = yhi[PZ, z:z + 1, :]
    for z in range(PZ):
        g, zz = z // GROUP, z % GROUP
        for t in range(PY // 8):
            v = piece(blocks, z, t)
            row = zz * PY + t * 8
            both = jnp.where(columns(lane, (g + 7) % 8), xlo[row:row + 8, :], xhi[row:row + 8, :])
            both = roll(both, -16 * g)
            tiles[0, z, t * 8:t * 8 + 8, :] = jnp.where(lane >= 112, both, v)
            tiles[1, z, t * 8:t * 8 + 8, :] = jnp.where(lane < 16, both, v)

    def element(ey, carry):
        warp_element(summed, tiles.at[0], ey, 0, warped)
        warp_element(summed, tiles.at[1], ey, 7, warped)
        return carry

    lax.fori_loop(0, 4, element, 0)
    middle = (lane >= 16) & (lane < 112)

    def rows(step, carry):
        y = pl.multiple_of(step * 8, 8)
        low = pltpu.roll(xlo[GROUP * PY:, :], (8 - step) % 8 * 16, 1)
        high = pltpu.roll(xhi[GROUP * PY:, :], (8 - step) % 8 * 16, 1)
        sums = [[None] * 6 for _ in range(3)]
        sums_r = [[None] * 3 for _ in range(2)]

        def add(where, k, i, term):
            where[k][i] = term if where[k][i] is None else where[k][i] + term

        for z in range(BZ):
            g, here = slopes(pad, low, high, z, y, lane)
            for p, (c, d) in enumerate(PAIRS):
                product = g[c] * g[d]
                for k in range(3):
                    add(sums, k, p, product * float(_SQ[k][z]))
            moved = jnp.where(middle, inside[z, pl.ds(y, 8), :], warped[z, pl.ds(y, 8), :])
            mismatch = here - moved
            for c in range(3):
                product = g[c] * mismatch
                for k in range(2):
                    add(sums_r, k, c, product * float(_LIN[k][z]))
        for k in range(3):
            for p in range(6):
                acc_k[k, pl.ds(p * BY + y, 8), :] = sums[k][p]
        for k in range(2):
            for c in range(3):
                acc_r[k, pl.ds(c * BY + y, 8), :] = sums_r[k][c]
        return carry

    lax.fori_loop(0, BY // 8, rows, 0)

    def contract(left, fields, right):
        half = jnp.dot(left[...], fields, precision=HI, preferred_element_type=F32)
        return jnp.dot(half, right[...], precision=HI, preferred_element_type=F32)

    packed = [jnp.zeros((8, BX), F32) for _ in range(5)]
    for k in range(3):
        full = contract(left_k, acc_k[k], right_k)
        kz = 1 if k == 2 else 0
        for q in range(9):
            ky, jy = (0, q) if q < 5 else (1, q - 5)
            rows_ = full[q * 8:q * 8 + 8]
            for kx in range(2):
                if kz == 0:
                    row, base = ky * 2 + kx, BLK * k
                elif ky == 1:
                    row, base = 1 - kx, 90
                else:
                    row, base = 2 + kx, 81
                source = 0 if kx == 0 else 9
                width = 9 if kx == 0 else 8
                part = jnp.where((lane >= source) & (lane < source + width), rows_, 0.0)
                packed[row] = packed[row] + roll(part, base + jy * JX - source)
    for k in range(2):
        full = contract(left_r, acc_r[k], right_r)
        for jy in range(JY):
            part = jnp.where(lane < JX, full[jy * 8:jy * 8 + 8], 0.0)
            packed[4] = packed[4] + roll(part, BLK * k + jy * JX)
    for row in range(4):
        out[row * 6:row * 6 + 6, :] = packed[row][0:6]
    out[KROWS:KROWS + 8, :] = packed[4]


def terms(summed, *arrays):
    return pl.pallas_call(
        terms_kernel,
        out_shape=jax.ShapeDtypeStruct((KROWS + 8, BX), F32),
        in_specs=[SMEM] + [VMEM] * 15,
        out_specs=VMEM,
        scratch_shapes=[
            pltpu.VMEM((BZ + 2, BY + 16, BX), F32),
            pltpu.VMEM((2, PZ, PY, BX), F32),
            pltpu.VMEM((BZ, BY, BX), F32),
            pltpu.VMEM((3, 6 * BY, BX), F32),
            pltpu.VMEM((2, 3 * BY, BX), F32),
        ],
        compiler_params=grant(20),
        name="terms",
    )(summed, *arrays, jnp.asarray(LEFT_K), jnp.asarray(RIGHT_K),
      jnp.asarray(LEFT_R), jnp.asarray(RIGHT_R))


NZ = NGZ + 1
TILES = NZ * 2


SLOTS0 = 54 * TILES
SLOTS = SLOTS0 + 54 * 2 * NGZ


STEPS = (("gz", (1, 2, 3), False), ("gx", (2,), False), ("gy", (2, 4, 6), False), ("gx", (1, 3), True))
QUAD = NGZ * (KROWS + RROWS)


def units():
    held = [(0, 0)]
    for axis, partners, halved in STEPS[1:]:
        n = len(held) // 2
        groups = (held[:n], held[n:]) if halved else (held,) * len(partners)
        for group, s in zip(groups, partners):
            dx, dy = (s, 0) if axis == "gx" else (0, s)
            held = held + [(x ^ dx, y ^ dy) for x, y in group]
    assert sorted(held) == [(x, y) for x in range(NGX) for y in range(0, NGY, 2)]
    return held


def brick(buf, where, gz, gx, row, rhs):
    dz, dx = gz ^ where[0], gx ^ where[2]
    first = NGZ * KROWS + dz * RROWS if rhs else dz * KROWS
    start = pl.multiple_of((((dx & 1) * 2 + (dx >> 1)) * QUAD + first + row) * 8, 8)
    return buf[pl.ds(start, 8), :]


def stencil_slot(kz, oy, ox, pair, i):
    slot = ((oy + 1) * 3 + ox + 1) * 6 + pair
    return slot * TILES + i if kz == 0 else SLOTS0 + slot * 2 * NGZ + i


def planes(s, width):
    lane = lanes()
    zero = jnp.zeros((8, BX), F32)
    out = []
    for z in range(NZ):
        for h in range(2):
            e, o = zero, zero
            if z < NGZ:
                e = s[z][2 * h]
                o = roll(s[z][2 * h + 1], BLK)
            if z > 0:
                e = e + roll(s[z - 1][2 * h], -BLK)
                o = o + s[z - 1][2 * h + 1]
            odd = (lane >= BLK) & (lane < BLK + width)
            out.append(jnp.where(lane < width, e, jnp.where(odd, o, zero)))
    return out


def edges(s, base, width):
    lane = lanes()
    out = []
    for z in range(NGZ):
        for h in range(2):
            e = roll(s[z][2 * h], -base)
            o = roll(s[z][2 * h + 1], BLK - base)
            odd = (lane >= BLK) & (lane < BLK + width)
            out.append(jnp.where(lane < width, e, jnp.where(odd, o, 0.0)))
    return out


def cg_kernel(
    where, part0, part1, out_x, out_r, buf, stencil, shifted, xs, rs, ys,
):
    own_z, own_y, own_x = where[0], where[1], where[2]
    for side, part in enumerate((part0, part1)):
        for i, (dx, dy) in enumerate(units()):
            gy = own_y ^ (side + dy)
            place = (dx & 1) * 2 + (dx >> 1)
            for r in range(0, QUAD, 8):
                buf[pl.ds((place * QUAD + r) * 8 + gy, 8, stride=8), :] = (
                    part[i * QUAD + r:i * QUAD + r + 8, :])

    def build(pair, carry):
        for row in range(4):
            s = [[brick(buf, where, gz, gx, row * 6 + pair, False) for gx in range(NGX)]
                 for gz in range(NGZ)]
            upper = (1, 1, 0, 0)[row]
            sides = (
                (0, row >> 1, row & 1, planes(s, 36 if row >> 1 else BLK)),
                (1, upper, (1, 0, 0, 1)[row],
                 edges(s, 90 if upper else 81, 36 if upper else BLK)),
            )
            for kz, ky, kx, field in sides:
                for oy in ((0,) if ky == 0 else (1, -1)):
                    for ox in ((0,) if kx == 0 else (1, -1)):
                        amount = (JX if oy == -1 else 0) + (1 if ox == 1 else 0)
                        for i, v in enumerate(field):
                            stencil[stencil_slot(kz, oy, ox, pair, i)] = roll(v, amount)
        return carry

    lax.fori_loop(0, 6, build, 0)
    lane = lanes()
    sub = lax.broadcasted_iota(jnp.int32, (8, BX), 0)
    even, odd = lane < BLK, (lane >= BLK) & (lane < 2 * BLK)
    zero = jnp.zeros((8, BX), F32)

    def fold(y0, y1):
        a = y0 + jnp.where(m_odd0, roll(y0, 37), 0.0) + jnp.where(m_even8, roll(y0, -37), 0.0)
        b = y1 + jnp.where(m_odd0, roll(y1, 37), 0.0) + jnp.where(m_even8, roll(y1, -37), 0.0)
        a = a + jnp.where(m_odd8, roll(y1, 53), 0.0)
        b = b + jnp.where(m_even0, roll(y0, -53), 0.0)
        out = []
        for v in (a, b):
            up = roll(roll(v, 36), 7, 0)
            down = roll(roll(v, -36), 1, 0)
            out.append(v + jnp.where(m_top, up, 0.0) + jnp.where(m_bottom, down, 0.0))
        return out

    inside = lax.rem(lane, BLK)
    jy = inside // JX
    jx = lax.rem(inside, JX)
    m_odd0, m_odd8 = odd & (jx == 0), odd & (jx == 8)
    m_even0, m_even8 = even & (jx == 0), even & (jx == 8)
    valid = lane < 2 * BLK
    m_top = valid & (jy == 4) & (sub < 7)
    m_bottom = valid & (jy == 0) & (sub > 0)
    base = valid & ((jy < 4) | (sub == 7))
    owner = (
        jnp.where(base & (jx < 8), 1.0, 0.0),
        jnp.where(base & ((jx < 8) | odd), 1.0, 0.0),
    )

    def total(v):
        return jnp.sum(jnp.sum(v, axis=1, keepdims=True), axis=0, keepdims=True)

    part = [zero, zero]
    for c in range(3):
        s = [[brick(buf, where, gz, gx, c, True) for gx in range(NGX)] for gz in range(NGZ)]
        field = planes(s, BLK)
        for z in range(NZ):
            pair_ = fold(field[2 * z], field[2 * z + 1])
            for h in range(2):
                v = pair_[h]
                i = 2 * z + h
                rs[c, i] = v
                xs[c, i] = zero
                shifted[c, 1, i] = v
                shifted[c, 0, i] = roll(v, JX)
                shifted[c, 2, i] = roll(v, -JX)
                part[h] = part[h] + v * v
    norm = total(part[0] * owner[0] + part[1] * owner[1])

    def step(_, norm_now):
        part = [zero, zero]
        for z in range(NZ):
            for h in range(2):
                sums = [[None] * 3 for _ in range(3)]
                for oz in (-1, 0, 1):
                    if not 0 <= z + oz < NZ:
                        continue
                    kz = 0 if oz == 0 else 1
                    kt = (z - 1 if oz == -1 else z) * 2 + h
                    for oy in range(3):
                        p = [shifted[d, oy, (z + oz) * 2 + h] for d in range(3)]
                        for ox in range(3):
                            k = [stencil[stencil_slot(kz, oy - 1, ox - 1, q, kt)] for q in range(6)]
                            for c in range(3):
                                for d in range(3):
                                    term = k[PAIR_OF[min(c, d), max(c, d)]] * p[d]
                                    old = sums[c][ox]
                                    sums[c][ox] = term if old is None else old + term
                for c in range(3):
                    ys[c, 2 * z + h] = sums[c][1] + roll(sums[c][0], 1) + roll(sums[c][2], -1)
            for c in range(3):
                pair_ = fold(ys[c, 2 * z], ys[c, 2 * z + 1])
                for h in range(2):
                    i = 2 * z + h
                    p = shifted[c, 1, i]
                    v = pair_[h] + DAMPING * p
                    ys[c, i] = v
                    part[h] = part[h] + v * p
        alpha = norm_now / total(part[0] * owner[0] + part[1] * owner[1])
        part = [zero, zero]
        for c in range(3):
            for i in range(TILES):
                xs[c, i] = xs[c, i] + alpha * shifted[c, 1, i]
                r = rs[c, i] - alpha * ys[c, i]
                rs[c, i] = r
                part[i % 2] = part[i % 2] + r * r
        norm_next = total(part[0] * owner[0] + part[1] * owner[1])
        beta = norm_next / norm_now
        for c in range(3):
            for i in range(TILES):
                p = rs[c, i] + beta * shifted[c, 1, i]
                shifted[c, 1, i] = p
                shifted[c, 0, i] = roll(p, JX)
                shifted[c, 2, i] = roll(p, -JX)
        return norm_next

    lax.fori_loop(0, CGSTEPS, step, norm)

    half, side = own_x >> 1, own_x & 1
    turn = jnp.where(side == 1, BX - BLK, 0)
    for src, dst, scale in ((xs, out_x, float(QUANTUM)), (rs, out_r, 1.0)):
        for c in range(3):
            for jz in range(2):
                v = src[c, (own_z + jz) * 2 + half]
                v = pltpu.roll(pltpu.roll(v, turn, 1), (8 - own_y) & 7, 0) * scale
                tile = zero
                for j in range(JY):
                    row = roll(roll(v, -j * JX), j, 0)
                    tile = jnp.where(sub == j, row, tile)
                dst[c, :, jz, :] = tile[0:JY, 0:JX]


def solve(where, parts):
    shape = jax.ShapeDtypeStruct((3, JY, 2, JX), F32)
    field = pltpu.VMEM((3, TILES, 8, BX), F32)
    return pl.pallas_call(
        cg_kernel,
        out_shape=[shape, shape],
        in_specs=[SMEM] + [VMEM] * 2,
        out_specs=[VMEM, VMEM],
        scratch_shapes=[
            pltpu.VMEM((NGX * QUAD * 8, BX), F32),
            pltpu.VMEM((SLOTS, 8, BX), F32),
            pltpu.VMEM((3, 3, TILES, 8, BX), F32),
            field, field, field,
        ],
        compiler_params=grant(20),
        name="cg",
    )(where, *parts)


def partner(x, axis, s):
    return lax.ppermute(x, axis, [(k ^ s, k) for k in range(lax.axis_size(axis))])


def exchange(a, b, axis):
    n = lax.axis_size(axis)
    outer = [(k, k + 1) for k in range(1, n - 1, 2)]
    b = lax.ppermute(b, axis, outer + [(j, i) for i, j in outer])
    return partner(a, axis, 1), b


def sorted_sides(a, b, axis):
    even = lax.axis_index(axis) % 2 == 0
    return jnp.where(even, b, a), jnp.where(even, a, b)


def halo(low, high, axis):
    even = lax.axis_index(axis) % 2 == 0
    return sorted_sides(
        *exchange(jnp.where(even, high, low), jnp.where(even, low, high), axis), axis)


def along_y(up, down):
    even = lax.axis_index("gy") % 2 == 0
    out = [(k, k + 1) for k in range(1, NGY - 1, 2)]
    near = [(k, k ^ 1) for k in range(NGY)]
    outer = jnp.where(even, down, up)
    up, down, _ = lax.optimization_barrier((up, down, outer))
    outer = lax.ppermute(outer, "gy", out + [(b, a) for a, b in out])
    inner_ = lax.ppermute(jnp.where(even, up, down), "gy", near)
    return jnp.where(even, outer, inner_), jnp.where(even, inner_, outer)


def gather(rows):
    for i, (axis, partners, halved) in enumerate(STEPS):
        n = rows.shape[0] // 2
        held = (rows[:n], rows[n:]) if halved else (rows,) * len(partners)
        theirs = [partner(h, axis, s) for h, s in zip(held, partners)]
        if i == 0:
            k, r = KROWS, KROWS + RROWS
            theirs = [v[:k] for v in [rows] + theirs] + [v[k:r] for v in [rows] + theirs]
            rows = jnp.concatenate(theirs, 0)
        else:
            rows = jnp.concatenate([rows] + theirs, 0)
    return rows, partner(rows, "gy", 1)


def element_sums(nodes):
    low = nodes[:, 0] + nodes[:, 1]
    low = low[:, :-1] + low[:, 1:]
    low = low[:, :, :-1] + low[:, :, 1:]
    return low.reshape(96)


def per_device(ref_image, deformed_image, nodal_disp):
    dza, dzb = exchange(deformed_image, deformed_image, "gz")
    rzlo, rzhi = halo(ref_image[:1], ref_image[BZ - 1:], "gz")
    summed = element_sums(nodal_disp)
    where = jnp.stack([lax.axis_index("gz"), lax.axis_index("gy"), lax.axis_index("gx")])
    dza, dzb, rzlo, rzhi, summed = lax.optimization_barrier((dza, dzb, rzlo, rzhi, summed))
    dzlo, dzhi = sorted_sides(dza, dzb, "gz")
    planes_ = (dzlo, deformed_image, dzhi)
    up = [v[:, BY - E:, :] for v in planes_] + [ref_image[:, BY - 1, :][None]]
    down = [v[:, :E, :] for v in planes_] + [ref_image[:, 0, :][None]]
    dylo, dyhi = along_y(jnp.concatenate(up, 0), jnp.concatenate(down, 0))
    blocks = (deformed_image, dzlo, dzhi, dylo, dyhi)
    first, last = strips(ref_image, *blocks)
    dxlo, dxhi = halo(first, last, "gx")
    inside = inner(lax.optimization_barrier((summed, first))[0], *blocks)
    rows = terms(summed, ref_image, rzlo, rzhi, *blocks, dxlo, dxhi, inside)
    return tuple(jnp.swapaxes(v, 1, 2) for v in solve(where, gather(rows)))


def solution(mesh):
    spec3 = P("gz", "gy", "gx")
    spec4 = P(None, "gz", "gy", "gx")
    return jax.shard_map(
        per_device, mesh=mesh, in_specs=(spec3, spec3, spec4), out_specs=(spec4, spec4),
        check_vma=False,
    )
```

```python
import jax
import jax.numpy as jnp
import numpy as np
from jax import lax
from jax.experimental import pallas as pl
from jax.experimental.pallas import tpu as pltpu
from jax.sharding import PartitionSpec as P

E = 16
CGSTEPS = 8
QUANTUM = 64
DAMPING = 0.5
BZ, BY, BX = 16, 64, 128
NGZ, NGY, NGX = 4, 8, 4
JY, JX = 5, 9
BLK = JY * JX
HI = lax.Precision.HIGHEST
PAIRS = ((0, 0), (0, 1), (0, 2), (1, 1), (1, 2), (2, 2))
PAIR_OF = {(0, 0): 0, (0, 1): 1, (0, 2): 2, (1, 1): 3, (1, 2): 4, (2, 2): 5}
KROWS = 24
RROWS = 4
F32 = jnp.float32

_T = (np.arange(E) + 0.5) / E
_W0, _W1 = 1.0 - _T, _T


def _place(kinds, count):
    low, high, mixed = kinds
    rows = np.zeros((count + 1 + (count if mixed is not None else 0), count * E), np.float32)
    for e in range(count):
        rows[e, e * E:(e + 1) * E] += low
        rows[e + 1, e * E:(e + 1) * E] += high
        if mixed is not None:
            rows[count + 1 + e, e * E:(e + 1) * E] = mixed
    return rows


def _left(rows, fields):
    out = np.zeros((rows.shape[0] * 8, fields * BY), np.float32)
    for q in range(rows.shape[0]):
        for f in range(fields):
            out[q * 8 + f, f * BY:(f + 1) * BY] = rows[q]
    return out


def _right(rows, scale):
    out = np.zeros((BX, BX), np.float32)
    out[:, :rows.shape[0]] = rows.T * scale
    return out


_SQ = (_W0 * _W0, _W1 * _W1, _W0 * _W1)
_LIN = (_W0, _W1, None)
LEFT_K = _left(_place(_SQ, 4), 6)
RIGHT_K = _right(_place(_SQ, 8), 0.25 / E**2)
LEFT_R = _left(_place(_LIN, 4), 3)
RIGHT_R = _right(_place(_LIN, 8), 0.5 / E**2)


def lanes(shape=(8, BX)):
    return lax.broadcasted_iota(jnp.int32, shape, len(shape) - 1)


def roll(x, amount, axis=1):
    size = x.shape[axis]
    if isinstance(amount, int):
        amount %= size
        if amount == 0:
            return x
    return pltpu.roll(x, amount, axis)


VMEM = pl.BlockSpec(memory_space=pltpu.VMEM)
SMEM = pl.BlockSpec(memory_space=pltpu.SMEM)


def grant(mib):
    return pltpu.CompilerParams(vmem_limit_bytes=mib << 20)


PZ, PY = 3 * E, BY + 2 * E
GROUP = PZ // 8
STRIP = GROUP * PY + 8


def piece(blocks, z, tile):
    mid, zlo, zhi, ylo, yhi = blocks
    if tile < 2:
        return ylo[z, tile * 8:tile * 8 + 8, :]
    if tile >= 10:
        return yhi[z, (tile - 10) * 8:(tile - 10) * 8 + 8, :]
    return (zlo, mid, zhi)[z // E][z % E, (tile - 2) * 8:(tile - 2) * 8 + 8, :]


def columns(lane, g):
    return (lane >= 16 * g) & (lane < 16 * g + 16)


def strips_kernel(ref, mid, zlo, zhi, ylo, yhi, first, last):
    blocks = (mid, zlo, zhi, ylo, yhi)
    lane = lanes()
    for zz in range(GROUP):
        for tile in range(PY // 8):
            a = jnp.zeros((8, BX), F32)
            b = jnp.zeros((8, BX), F32)
            for g in range(8):
                v = piece(blocks, g * GROUP + zz, tile)
                v = roll(v, 16 * g)
                a = jnp.where(columns(lane, g), v, a)
                b = jnp.where(columns(lane, (g + 7) % 8), v, b)
            row = zz * PY + tile * 8
            first[row:row + 8, :] = a
            last[row:row + 8, :] = b
    a = jnp.zeros((8, BX), F32)
    b = jnp.zeros((8, BX), F32)
    for tile in range(BY // 8):
        for z in range(BZ):
            v = ref[z, tile * 8:tile * 8 + 8, :]
            to = 16 * tile + z
            a = jnp.where(lane == to, roll(v, to), a)
            b = jnp.where(lane == to, roll(v, to + 1), b)
    first[GROUP * PY:, :] = a
    last[GROUP * PY:, :] = b


def strips(ref, *blocks):
    shape = jax.ShapeDtypeStruct((STRIP, BX), F32)
    return pl.pallas_call(
        strips_kernel,
        out_shape=[shape, shape],
        in_specs=[VMEM] * 6,
        out_specs=[VMEM] * 2,
        compiler_params=grant(8),
        name="strips",
    )(ref, *blocks)


def warp_element(summed, tile, ey, ex, warped):
    lane = lanes((E, BX))
    e = ey * 8 + ex
    sz, sy, sx = summed[e], summed[32 + e], summed[64 + e]
    whole_z = lax.shift_right_arithmetic(sz, 9)
    whole_y = lax.shift_right_arithmetic(sy, 9)
    whole_x = lax.shift_right_arithmetic(sx, 9)
    scale = 1.0 / (8.0 * QUANTUM)
    fz = (sz & 511).astype(F32) * scale
    fy = (sy & 511).astype(F32) * scale
    fx = (sx & 511).astype(F32) * scale
    start_z = whole_z + E
    start_y = whole_y + E + ey * E
    turn = jnp.where(whole_x > 0, BX - whole_x, -whole_x)
    mask = (lane >= ex * 16) & (lane < ex * 16 + 16)
    row = pl.multiple_of(ey * E, E)

    def plane(k):
        a = tile[start_z + k, pl.ds(start_y, E), :]
        b = tile[start_z + k, pl.ds(start_y + 1, E), :]
        return (1.0 - fy) * a + fy * b

    below = plane(0)
    for k in range(E):
        above = plane(k + 1)
        v = (1.0 - fz) * below + fz * above
        v = pltpu.roll(v, turn, 1)
        v = (1.0 - fx) * v + fx * roll(v, BX - 1)
        pltpu.store(warped.at[k, pl.ds(row, E), :], v, mask=mask)
        below = above


def inner_kernel(summed, mid, zlo, zhi, ylo, yhi, warped, tile):
    blocks = (mid, zlo, zhi, ylo, yhi)
    for z in range(PZ):
        for t in range(PY // 8):
            tile[z, t * 8:t * 8 + 8, :] = piece(blocks, z, t)

    def pair(i, carry):
        for ex in range(2):
            warp_element(summed, tile, i // 3, 1 + 2 * (i % 3) + ex, warped)
        return carry

    lax.fori_loop(0, 12, pair, 0)


def inner(summed, *blocks):
    return pl.pallas_call(
        inner_kernel,
        out_shape=jax.ShapeDtypeStruct((BZ, BY, BX), F32),
        in_specs=[SMEM] + [VMEM] * 5,
        out_specs=VMEM,
        scratch_shapes=[pltpu.VMEM((PZ, PY, BX), F32)],
        compiler_params=grant(10),
        name="inner",
    )(summed, *blocks)


def slopes(pad, xlo, xhi, z, y, lane):
    here = pad[z + 1, pl.ds(8 + y, 8), :]
    along_z = pad[z + 2, pl.ds(8 + y, 8), :] - pad[z, pl.ds(8 + y, 8), :]
    along_y = pad[z + 1, pl.ds(9 + y, 8), :] - pad[z + 1, pl.ds(7 + y, 8), :]
    after_ = jnp.where(lane == BX - 1, roll(xhi, BX - 1 - z), roll(here, BX - 1))
    before = jnp.where(lane == 0, roll(xlo, -z), roll(here, 1))
    return (along_z, along_y, after_ - before), here


def terms_kernel(
    summed, ref, rzlo, rzhi, mid, zlo, zhi, ylo, yhi, xlo, xhi, inside,
    left_k, right_k, left_r, right_r, out, pad, tiles, warped, acc_k, acc_r,
):
    blocks = (mid, zlo, zhi, ylo, yhi)
    lane = lanes()
    pad[1:BZ + 1, 8:8 + BY, :] = ref[...]
    pad[0:1, 8:8 + BY, :] = rzlo[...]
    pad[BZ + 1:BZ + 2, 8:8 + BY, :] = rzhi[...]
    for z in range(BZ):
        pad[z + 1, 7:8, :] = ylo[PZ, z:z + 1, :]
        pad[z + 1, 8 + BY:9 + BY, :] = yhi[PZ, z:z + 1, :]
    for z in range(PZ):
        g, zz = z // GROUP, z % GROUP
        for t in range(PY // 8):
            v = piece(blocks, z, t)
            row = zz * PY + t * 8
            both = jnp.where(columns(lane, (g + 7) % 8), xlo[row:row + 8, :], xhi[row:row + 8, :])
            both = roll(both, -16 * g)
            tiles[0, z, t * 8:t * 8 + 8, :] = jnp.where(lane >= 112, both, v)
            tiles[1, z, t * 8:t * 8 + 8, :] = jnp.where(lane < 16, both, v)

    def element(ey, carry):
        warp_element(summed, tiles.at[0], ey, 0, warped)
        warp_element(summed, tiles.at[1], ey, 7, warped)
        return carry

    lax.fori_loop(0, 4, element, 0)
    middle = (lane >= 16) & (lane < 112)

    def rows(step, carry):
        y = pl.multiple_of(step * 8, 8)
        low = pltpu.roll(xlo[GROUP * PY:, :], (8 - step) % 8 * 16, 1)
        high = pltpu.roll(xhi[GROUP * PY:, :], (8 - step) % 8 * 16, 1)
        sums = [[None] * 6 for _ in range(3)]
        sums_r = [[None] * 3 for _ in range(2)]

        def add(where, k, i, term):
            where[k][i] = term if where[k][i] is None else where[k][i] + term

        for z in range(BZ):
            g, here = slopes(pad, low, high, z, y, lane)
            for p, (c, d) in enumerate(PAIRS):
                product = g[c] * g[d]
                for k in range(3):
                    add(sums, k, p, product * float(_SQ[k][z]))
            moved = jnp.where(middle, inside[z, pl.ds(y, 8), :], warped[z, pl.ds(y, 8), :])
            mismatch = here - moved
            for c in range(3):
                product = g[c] * mismatch
                for k in range(2):
                    add(sums_r, k, c, product * float(_LIN[k][z]))
        for k in range(3):
            for p in range(6):
                acc_k[k, pl.ds(p * BY + y, 8), :] = sums[k][p]
        for k in range(2):
            for c in range(3):
                acc_r[k, pl.ds(c * BY + y, 8), :] = sums_r[k][c]
        return carry

    lax.fori_loop(0, BY // 8, rows, 0)

    def contract(left, fields, count, right):
        halves = [jnp.dot(left[...], fields[k], precision=HI, preferred_element_type=F32)
                  for k in range(count)]
        full = jnp.dot(jnp.concatenate(halves, 0), right[...], precision=HI,
                       preferred_element_type=F32)
        n = left.shape[0]
        return [full[k * n:k * n + n] for k in range(count)]

    fulls_k = contract(left_k, acc_k, 3, right_k)
    fulls_r = contract(left_r, acc_r, 2, right_r)
    packed = [jnp.zeros((8, BX), F32) for _ in range(5)]
    for k in range(3):
        full = fulls_k[k]
        kz = 1 if k == 2 else 0
        for q in range(9):
            ky, jy = (0, q) if q < 5 else (1, q - 5)
            rows_ = full[q * 8:q * 8 + 8]
            for kx in range(2):
                if kz == 0:
                    row, base = ky * 2 + kx, BLK * k
                elif ky == 1:
                    row, base = 1 - kx, 90
                else:
                    row, base = 2 + kx, 81
                source = 0 if kx == 0 else 9
                width = 9 if kx == 0 else 8
                part = jnp.where((lane >= source) & (lane < source + width), rows_, 0.0)
                packed[row] = packed[row] + roll(part, base + jy * JX - source)
    for k in range(2):
        full = fulls_r[k]
        for jy in range(JY):
            part = jnp.where(lane < JX, full[jy * 8:jy * 8 + 8], 0.0)
            packed[4] = packed[4] + roll(part, BLK * k + jy * JX)
    for row in range(4):
        out[row * 6:row * 6 + 6, :] = packed[row][0:6]
    out[KROWS:KROWS + 8, :] = packed[4]


def terms(summed, *arrays):
    return pl.pallas_call(
        terms_kernel,
        out_shape=jax.ShapeDtypeStruct((KROWS + 8, BX), F32),
        in_specs=[SMEM] + [VMEM] * 15,
        out_specs=VMEM,
        scratch_shapes=[
            pltpu.VMEM((BZ + 2, BY + 16, BX), F32),
            pltpu.VMEM((2, PZ, PY, BX), F32),
            pltpu.VMEM((BZ, BY, BX), F32),
            pltpu.VMEM((3, 6 * BY, BX), F32),
            pltpu.VMEM((2, 3 * BY, BX), F32),
        ],
        compiler_params=grant(20),
        name="terms",
    )(summed, *arrays, jnp.asarray(LEFT_K), jnp.asarray(RIGHT_K),
      jnp.asarray(LEFT_R), jnp.asarray(RIGHT_R))


NZ = NGZ + 1
TILES = NZ * 2


SLOTS0 = 54 * TILES
SLOTS = SLOTS0 + 54 * 2 * NGZ


STEPS = (("gz", (1, 2, 3), False), ("gx", (2,), False), ("gy", (2, 4, 6), False), ("gx", (1, 3), True))
QUAD = NGZ * (KROWS + RROWS)


def units():
    held = [(0, 0)]
    for axis, partners, halved in STEPS[1:]:
        n = len(held) // 2
        groups = (held[:n], held[n:]) if halved else (held,) * len(partners)
        for group, s in zip(groups, partners):
            dx, dy = (s, 0) if axis == "gx" else (0, s)
            held = held + [(x ^ dx, y ^ dy) for x, y in group]
    assert sorted(held) == [(x, y) for x in range(NGX) for y in range(0, NGY, 2)]
    return held


def brick(buf, where, gz, gx, row, rhs):
    dz, dx = gz ^ where[0], gx ^ where[2]
    first = NGZ * KROWS + dz * RROWS if rhs else dz * KROWS
    start = pl.multiple_of((((dx & 1) * 2 + (dx >> 1)) * QUAD + first + row) * 8, 8)
    return buf[pl.ds(start, 8), :]


def stencil_slot(kz, oy, ox, pair, i):
    slot = ((oy + 1) * 3 + ox + 1) * 6 + pair
    return slot * TILES + i if kz == 0 else SLOTS0 + slot * 2 * NGZ + i


def planes(s, width):
    lane = lanes()
    zero = jnp.zeros((8, BX), F32)
    out = []
    for z in range(NZ):
        for h in range(2):
            e, o = zero, zero
            if z < NGZ:
                e = s[z][2 * h]
                o = roll(s[z][2 * h + 1], BLK)
            if z > 0:
                e = e + roll(s[z - 1][2 * h], -BLK)
                o = o + s[z - 1][2 * h + 1]
            odd = (lane >= BLK) & (lane < BLK + width)
            out.append(jnp.where(lane < width, e, jnp.where(odd, o, zero)))
    return out


def edges(s, base, width):
    lane = lanes()
    out = []
    for z in range(NGZ):
        for h in range(2):
            e = roll(s[z][2 * h], -base)
            o = roll(s[z][2 * h + 1], BLK - base)
            odd = (lane >= BLK) & (lane < BLK + width)
            out.append(jnp.where(lane < width, e, jnp.where(odd, o, 0.0)))
    return out


def cg_kernel(
    where, part0, part1, out_x, out_r, buf, stencil, shifted, xs, rs, ys,
):
    own_z, own_y, own_x = where[0], where[1], where[2]
    for side, part in enumerate((part0, part1)):
        for i, (dx, dy) in enumerate(units()):
            gy = own_y ^ (side + dy)
            place = (dx & 1) * 2 + (dx >> 1)
            for r in range(0, QUAD, 8):
                buf[pl.ds((place * QUAD + r) * 8 + gy, 8, stride=8), :] = (
                    part[i * QUAD + r:i * QUAD + r + 8, :])

    def build(pair, carry):
        for row in range(4):
            s = [[brick(buf, where, gz, gx, row * 6 + pair, False) for gx in range(NGX)]
                 for gz in range(NGZ)]
            upper = (1, 1, 0, 0)[row]
            sides = (
                (0, row >> 1, row & 1, planes(s, 36 if row >> 1 else BLK)),
                (1, upper, (1, 0, 0, 1)[row],
                 edges(s, 90 if upper else 81, 36 if upper else BLK)),
            )
            for kz, ky, kx, field in sides:
                for oy in ((0,) if ky == 0 else (1, -1)):
                    for ox in ((0,) if kx == 0 else (1, -1)):
                        amount = (JX if oy == -1 else 0) + (1 if ox == 1 else 0)
                        for i, v in enumerate(field):
                            stencil[stencil_slot(kz, oy, ox, pair, i)] = roll(v, amount)
        return carry

    lax.fori_loop(0, 6, build, 0)
    lane = lanes()
    sub = lax.broadcasted_iota(jnp.int32, (8, BX), 0)
    even, odd = lane < BLK, (lane >= BLK) & (lane < 2 * BLK)
    zero = jnp.zeros((8, BX), F32)

    def fold(y0, y1):
        a = y0 + jnp.where(m_odd0, roll(y0, 37), 0.0) + jnp.where(m_even8, roll(y0, -37), 0.0)
        b = y1 + jnp.where(m_odd0, roll(y1, 37), 0.0) + jnp.where(m_even8, roll(y1, -37), 0.0)
        a = a + jnp.where(m_odd8, roll(y1, 53), 0.0)
        b = b + jnp.where(m_even0, roll(y0, -53), 0.0)
        out = []
        for v in (a, b):
            up = roll(roll(v, 36), 7, 0)
            down = roll(roll(v, -36), 1, 0)
            out.append(v + jnp.where(m_top, up, 0.0) + jnp.where(m_bottom, down, 0.0))
        return out

    inside = lax.rem(lane, BLK)
    jy = inside // JX
    jx = lax.rem(inside, JX)
    m_odd0, m_odd8 = odd & (jx == 0), odd & (jx == 8)
    m_even0, m_even8 = even & (jx == 0), even & (jx == 8)
    valid = lane < 2 * BLK
    m_top = valid & (jy == 4) & (sub < 7)
    m_bottom = valid & (jy == 0) & (sub > 0)
    base = valid & ((jy < 4) | (sub == 7))
    owner = (
        jnp.where(base & (jx < 8), 1.0, 0.0),
        jnp.where(base & ((jx < 8) | odd), 1.0, 0.0),
    )

    def total(v):
        return jnp.sum(jnp.sum(v, axis=1, keepdims=True), axis=0, keepdims=True)

    part = [zero, zero]
    for c in range(3):
        s = [[brick(buf, where, gz, gx, c, True) for gx in range(NGX)] for gz in range(NGZ)]
        field = planes(s, BLK)
        for z in range(NZ):
            pair_ = fold(field[2 * z], field[2 * z + 1])
            for h in range(2):
                v = pair_[h]
                i = 2 * z + h
                rs[c, i] = v
                xs[c, i] = zero
                shifted[c, 1, i] = v
                shifted[c, 0, i] = roll(v, JX)
                shifted[c, 2, i] = roll(v, -JX)
                part[h] = part[h] + v * v
    norm = total(part[0] * owner[0] + part[1] * owner[1])

    def step(_, norm_now):
        part = [zero, zero]
        for z in range(NZ):
            for h in range(2):
                sums = [[None] * 3 for _ in range(3)]
                for oz in (-1, 0, 1):
                    if not 0 <= z + oz < NZ:
                        continue
                    kz = 0 if oz == 0 else 1
                    kt = (z - 1 if oz == -1 else z) * 2 + h
                    for oy in range(3):
                        p = [shifted[d, oy, (z + oz) * 2 + h] for d in range(3)]
                        for ox in range(3):
                            k = [stencil[stencil_slot(kz, oy - 1, ox - 1, q, kt)] for q in range(6)]
                            for c in range(3):
                                for d in range(3):
                                    term = k[PAIR_OF[min(c, d), max(c, d)]] * p[d]
                                    old = sums[c][ox]
                                    sums[c][ox] = term if old is None else old + term
                for c in range(3):
                    ys[c, 2 * z + h] = sums[c][1] + roll(sums[c][0], 1) + roll(sums[c][2], -1)
            for c in range(3):
                pair_ = fold(ys[c, 2 * z], ys[c, 2 * z + 1])
                for h in range(2):
                    i = 2 * z + h
                    p = shifted[c, 1, i]
                    v = pair_[h] + DAMPING * p
                    ys[c, i] = v
                    part[h] = part[h] + v * p
        alpha = norm_now / total(part[0] * owner[0] + part[1] * owner[1])
        part = [zero, zero]
        for c in range(3):
            for i in range(TILES):
                xs[c, i] = xs[c, i] + alpha * shifted[c, 1, i]
                r = rs[c, i] - alpha * ys[c, i]
                rs[c, i] = r
                part[i % 2] = part[i % 2] + r * r
        norm_next = total(part[0] * owner[0] + part[1] * owner[1])
        beta = norm_next / norm_now
        for c in range(3):
            for i in range(TILES):
                p = rs[c, i] + beta * shifted[c, 1, i]
                shifted[c, 1, i] = p
                shifted[c, 0, i] = roll(p, JX)
                shifted[c, 2, i] = roll(p, -JX)
        return norm_next

    lax.fori_loop(0, CGSTEPS, step, norm)

    half, side = own_x >> 1, own_x & 1
    turn = jnp.where(side == 1, BX - BLK, 0)
    for src, dst, scale in ((xs, out_x, float(QUANTUM)), (rs, out_r, 1.0)):
        for c in range(3):
            for jz in range(2):
                v = src[c, (own_z + jz) * 2 + half]
                v = pltpu.roll(pltpu.roll(v, turn, 1), (8 - own_y) & 7, 0) * scale
                tile = zero
                for j in range(JY):
                    row = roll(roll(v, -j * JX), j, 0)
                    tile = jnp.where(sub == j, row, tile)
                dst[c, :, jz, :] = tile[0:JY, 0:JX]


def solve(where, parts):
    shape = jax.ShapeDtypeStruct((3, JY, 2, JX), F32)
    field = pltpu.VMEM((3, TILES, 8, BX), F32)
    return pl.pallas_call(
        cg_kernel,
        out_shape=[shape, shape],
        in_specs=[SMEM] + [VMEM] * 2,
        out_specs=[VMEM, VMEM],
        scratch_shapes=[
            pltpu.VMEM((NGX * QUAD * 8, BX), F32),
            pltpu.VMEM((SLOTS, 8, BX), F32),
            pltpu.VMEM((3, 3, TILES, 8, BX), F32),
            field, field, field,
        ],
        compiler_params=grant(20),
        name="cg",
    )(where, *parts)


def partner(x, axis, s):
    return lax.ppermute(x, axis, [(k ^ s, k) for k in range(lax.axis_size(axis))])


def exchange(a, b, axis):
    n = lax.axis_size(axis)
    outer = [(k, k + 1) for k in range(1, n - 1, 2)]
    b = lax.ppermute(b, axis, outer + [(j, i) for i, j in outer])
    return partner(a, axis, 1), b


def sorted_sides(a, b, axis):
    even = lax.axis_index(axis) % 2 == 0
    return jnp.where(even, b, a), jnp.where(even, a, b)


def halo(low, high, axis):
    even = lax.axis_index(axis) % 2 == 0
    return sorted_sides(
        *exchange(jnp.where(even, high, low), jnp.where(even, low, high), axis), axis)


def along_y(up, down):
    even = lax.axis_index("gy") % 2 == 0
    out = [(k, k + 1) for k in range(1, NGY - 1, 2)]
    near = [(k, k ^ 1) for k in range(NGY)]
    outer = jnp.where(even, down, up)
    up, down, _ = lax.optimization_barrier((up, down, outer))
    outer = lax.ppermute(outer, "gy", out + [(b, a) for a, b in out])
    inner_ = lax.ppermute(jnp.where(even, up, down), "gy", near)
    return jnp.where(even, outer, inner_), jnp.where(even, inner_, outer)


def gather(rows):
    for i, (axis, partners, halved) in enumerate(STEPS):
        n = rows.shape[0] // 2
        held = (rows[:n], rows[n:]) if halved else (rows,) * len(partners)
        theirs = [partner(h, axis, s) for h, s in zip(held, partners)]
        if i == 0:
            k, r = KROWS, KROWS + RROWS
            theirs = [v[:k] for v in [rows] + theirs] + [v[k:r] for v in [rows] + theirs]
            rows = jnp.concatenate(theirs, 0)
        else:
            rows = jnp.concatenate([rows] + theirs, 0)
    return rows, partner(rows, "gy", 1)


def element_sums(nodes):
    low = nodes[:, 0] + nodes[:, 1]
    low = low[:, :-1] + low[:, 1:]
    low = low[:, :, :-1] + low[:, :, 1:]
    return low.reshape(96)


def per_device(ref_image, deformed_image, nodal_disp):
    dza, dzb = exchange(deformed_image, deformed_image, "gz")
    rzlo, rzhi = halo(ref_image[:1], ref_image[BZ - 1:], "gz")
    summed = element_sums(nodal_disp)
    where = jnp.stack([lax.axis_index("gz"), lax.axis_index("gy"), lax.axis_index("gx")])
    dza, dzb, rzlo, rzhi, summed = lax.optimization_barrier((dza, dzb, rzlo, rzhi, summed))
    dzlo, dzhi = sorted_sides(dza, dzb, "gz")
    planes_ = (dzlo, deformed_image, dzhi)
    up = [v[:, BY - E:, :] for v in planes_] + [ref_image[:, BY - 1, :][None]]
    down = [v[:, :E, :] for v in planes_] + [ref_image[:, 0, :][None]]
    dylo, dyhi = along_y(jnp.concatenate(up, 0), jnp.concatenate(down, 0))
    blocks = (deformed_image, dzlo, dzhi, dylo, dyhi)
    first, last = strips(ref_image, *blocks)
    dxlo, dxhi = halo(first, last, "gx")
    inside = inner(lax.optimization_barrier((summed, first))[0], *blocks)
    rows = terms(summed, ref_image, rzlo, rzhi, *blocks, dxlo, dxhi, inside)
    return tuple(jnp.swapaxes(v, 1, 2) for v in solve(where, gather(rows)))


def solution(mesh):
    spec3 = P("gz", "gy", "gx")
    spec4 = P(None, "gz", "gy", "gx")
    return jax.shard_map(
        per_device, mesh=mesh, in_specs=(spec3, spec3, spec4), out_specs=(spec4, spec4),
        check_vma=False,
    )
```
